32 devices in a mesh: wide: 16 (over z, y, x), narrow: 2 (over core).
Axes of the slice: x: 2, y: 2, z: 4, core: 2. Of those that a mesh axis runs over, the one named last changes fastest.
Arguments:
- t_amps: bfloat16 [512, 32768], P('wide', 'narrow'), may hold values from -6 to 6
- v_blocks: bfloat16 [2, 16, 64, 128, 128], P('narrow', 'wide'), may hold values from -0.25 to 0.25
- block_pos: int32 [2, 16, 64], P('narrow', 'wide'), may hold values from 0 to 2047, as said below
- block_count: int32 [2, 16], P('narrow', 'wide'), may hold values from 24 to 64, as said below
Outputs:
- ladder: float32 [512, 32768], P('narrow', 'wide')
The draws below stay inside these ranges and needn't reach their ends.
Inputs may be any that keep to these rules, and one draw needn't show every extreme that they name: `block_pos`: within one tile the places of all 64 slots are distinct, and they lie in at most 64 distinct block rows. `block_count`: some tile holds exactly 64 stored blocks; loads are skewed, most tiles holding far fewer.
All inputs are finite; a program needn't handle non-finite values.
Results may differ from the reference program's by a relative error of at most 0.0003.
Values may be sent and summed in bfloat16 or wider, within the bound.
A program may use at most 320 MiB of HBM per device.

```python
import jax
import jax.numpy as jnp
from jax import lax

OP = 512
W = 32768
BS = 128
MAXB = 64
RB = 128
CB = 16
N_WIDE = 16
N_NARROW = 2


def draw_block_pos(key, part):
    half_rows = RB // 2
    keys = jax.random.split(jax.random.fold_in(key, 11), N_NARROW * N_WIDE)

    def one_tile(tile_key):
        row_key, place_key = jax.random.split(tile_key)
        row_scores = jax.random.randint(row_key, (RB,), 0, (1 << 30) // RB) * RB
        row_scores = row_scores + jnp.arange(RB, dtype=jnp.int32)
        chosen_rows = jnp.argsort(row_scores, stable=True)[:half_rows].astype(jnp.int32)
        total = half_rows * CB
        scores = jax.random.randint(place_key, (total,), 0, (1 << 30) // total) * total
        scores = scores + jnp.arange(total, dtype=jnp.int32)
        picked = jnp.argsort(scores, stable=True)[:MAXB].astype(jnp.int32)
        return chosen_rows[picked // CB] * CB + picked % CB
    places = jax.vmap(one_tile)(keys)
    return places.astype(jnp.int32).reshape(N_NARROW, N_WIDE, MAXB)


def draw_block_count(key, part):
    lowest = MAXB * 3 // 8
    draws = jax.random.randint(jax.random.fold_in(key, 23), (N_NARROW * N_WIDE,), 0, 1000)
    counts = lowest + draws * draws * (MAXB - lowest) // 998001
    fullest = jax.random.randint(jax.random.fold_in(key, 37), (), 0, N_NARROW * N_WIDE)
    counts = counts.at[fullest].set(MAXB)
    return counts.astype(jnp.int32).reshape(N_NARROW, N_WIDE)


def level_of(stream_key, shape, pieces, low, largest):
    level = 1.0
    for axis_at, parts in pieces:
        steps = jax.random.uniform(jax.random.fold_in(jax.random.fold_in(stream_key, 6), axis_at), (parts,), jnp.float32, low / len(pieces), largest / len(pieces))
        level = level * jnp.repeat(jnp.exp(steps), shape[axis_at] // parts).reshape((-1,) + (1,) * (len(shape) - 1 - axis_at))
    return level


def gaussian(key, dims, scale, most, pieces=(), kind=jnp.bfloat16):
    entries = jax.random.normal(key, dims, jnp.float32) * scale
    if len(pieces) > 0:
        entries = level_of(key, dims, pieces, -0.22, 0.18) * entries
    return jnp.clip(entries, min=-most, max=most).astype(kind)


def setup_inputs(seed: int = 0) -> dict:
    streams_of = jax.random.split(jax.random.key(seed), 5)
    t_amps = gaussian(streams_of[0], (OP, W), 1.0, 6.0, ((0, 16), (1, 2)))
    v_blocks = gaussian(streams_of[1], (N_NARROW, N_WIDE, MAXB, BS, BS), (MAXB * N_NARROW * BS // (2 * CB)) ** -0.5, 0.25, ((0, 2), (1, 16)))
    block_pos = draw_block_pos(jax.random.fold_in(streams_of[4], 71), 0)
    block_count = draw_block_count(jax.random.fold_in(streams_of[4], 71), 0)
    return dict(t_amps=t_amps, v_blocks=v_blocks, block_pos=block_pos, block_count=block_count)


def reference(t_amps, v_blocks, block_pos, block_count):
    slots = jnp.arange(MAXB, dtype=jnp.int32)
    col_ids = jnp.arange(CB, dtype=jnp.int32)

    def strip(w_index):
        def over_slice(accum, n_index):
            start = (n_index * (RB * BS)).astype(jnp.int32)
            t_part = lax.dynamic_slice_in_dim(t_amps, start, RB * BS, 1).astype(jnp.float32)
            t_part = t_part.reshape(OP, RB, BS)
            places = block_pos[n_index, w_index]
            row_index = places // CB
            col_index = places % CB
            live_mask = (slots < block_count[n_index, w_index]).astype(jnp.float32)
            stored = v_blocks[n_index, w_index].astype(jnp.float32) * live_mask[:, None, None]
            chosen = jnp.take(t_part, row_index, axis=1)
            products = jnp.einsum("ogk,gkm->ogm", chosen, stored, precision=lax.Precision.HIGHEST)
            one_hot = (col_index[:, None] == col_ids[None, :]).astype(jnp.float32)
            return accum + jnp.einsum("ogm,gc->ocm", products, one_hot, precision=lax.Precision.HIGHEST), None

        start_acc = jnp.zeros((OP, CB, BS), jnp.float32)
        accum, unused = lax.scan(over_slice, start_acc, jnp.arange(N_NARROW, dtype=jnp.int32))
        return accum.reshape(OP, CB * BS)

    strips = lax.map(strip, jnp.arange(N_WIDE, dtype=jnp.int32))
    return jnp.transpose(strips, (1, 0, 2)).reshape(OP, W)
```

```python
import functools

import jax
import jax.numpy as jnp
from jax import lax
from jax.experimental import pallas as pl
from jax.experimental.pallas import tpu as pltpu
from jax.sharding import PartitionSpec as P

MESH = pl.DeviceIdType.MESH
PIECES = 4


def dense_shards(width, t_amps, v_blocks, block_pos, block_count):
    stored = v_blocks[0, 0]
    places = block_pos[0, 0]
    slot_count = block_count[0, 0]
    block_size = stored.shape[1]
    slot_total = stored.shape[0]
    row_blocks = t_amps.shape[1] // block_size
    col_blocks = width // (lax.axis_size("wide") * block_size)
    live_mask = (jnp.arange(slot_total, dtype=jnp.int32) < slot_count).astype(jnp.bfloat16)
    masked = stored * live_mask[:, None, None]
    dense_tile = jnp.zeros((row_blocks * col_blocks, block_size, block_size), jnp.bfloat16)
    dense_tile = dense_tile.at[places].add(masked)
    dense_tile = dense_tile.reshape(row_blocks, col_blocks, block_size, block_size)
    dense_tile = jnp.transpose(dense_tile, (0, 2, 1, 3)).reshape(row_blocks * block_size, col_blocks * block_size)
    gathered = lax.all_gather(t_amps, "wide", axis=0, tiled=True)
    partial_sum = jnp.dot(gathered, dense_tile, preferred_element_type=jnp.float32)
    return lax.psum_scatter(partial_sum, "narrow", scatter_dimension=0, tiled=True)


def ladder_kernel(depth, t, v_tile, meta_v, out, *scratch):
    held = scratch[: (2 * depth - 1) * PIECES]
    bufs = [held[b * PIECES:(b + 1) * PIECES] for b in range(2 * depth - 1)]
    (v_own, v_other, meta_in, meta, meta_other, runs, part, core_in, y_out, own_out,
     lay_sem, local_sem, z_send, z_recv, x_send, x_recv, one_send, one_recv, core_send, core_recv, y_send, y_recv,
     own_sem) = scratch[(2 * depth - 1) * PIECES:]
    wide, core = lax.axis_index("wide"), lax.axis_index("narrow")
    z, y, x = wide // 4, (wide // 2) % 2, wide % 2
    up, down = (wide + 4, core), (wide - 4, core)
    across = (wide + 1 - 2 * x, core)
    beside = (wide + 2 - 4 * y, core)
    twin = (wide, 1 - core)
    half = depth // 2
    pieces, row_blocks, chunk, unused = t.shape
    v = v_tile.at[0, 0]
    slots, size = v.shape[0], v.shape[1]
    col_blocks = out.shape[-1] // size
    has_up, has_down = z < depth - 1, z > 0
    at_end = jnp.logical_or(z == 0, z == depth - 1)
    even = tuple(range(0, pieces, 2))
    odd = tuple(range(1, pieces, 2))
    halves = pieces // 2

    def copy(src, dst, send, recv, device):
        return pltpu.make_async_remote_copy(
            src_ref=src, dst_ref=dst, send_sem=send, recv_sem=recv, device_id=device, device_id_type=MESH
        )

    def guarded(cond, fn):
        if cond is None:
            fn()
        else:
            pl.when(cond)(fn)

    def both(a, b):
        return b if a is None else a if b is None else jnp.logical_and(a, b)

    def shards(k):
        if k == 0:
            return [(0, z, None, None)]
        return [(k, z - k, z >= k, 0), (depth - 1 + k, z + k, z + k < depth, 1)]

    def is_end(k, way):
        return at_end if k == 0 else (z == k) if way == 0 else (z + k == depth - 1)

    def onward(b, way):
        ups = [] if way == 1 or b == depth - 1 else [(0, up, has_up, b + 1)]
        downs = [] if way == 0 or b == 2 * depth - 2 else [(1, down, has_down, depth if b == 0 else b + 1)]
        return ups + downs

    def z_copy(b, kind, q, move):
        side = x if kind == 0 else 1 - x
        direction, device, unused, landing = move
        return copy(bufs[b][q].at[side], bufs[landing][q].at[side], z_send.at[direction, b, kind, q], z_recv.at[landing, kind, q], device)

    def x_copy(b, q):
        ref = bufs[b][q].at[x]
        return copy(ref, ref, x_send.at[b, q], x_recv.at[b, q], across)

    def z_wait(b, kind, q):
        ref = bufs[b][q].at[x if kind == 0 else 1 - x]
        copy(ref, ref, z_send.at[0, b, kind, q], z_recv.at[b, kind, q], up).wait_recv()

    def x_wait(b, q):
        ref = bufs[b][q].at[1 - x]
        copy(ref, ref, x_send.at[b, q], x_recv.at[b, q], across).wait_recv()

    lays = [pltpu.make_async_copy(t.at[q], bufs[0][q].at[x], lay_sem.at[q]) for q in range(pieces)]
    own_v = pltpu.make_async_copy(v, v_own, local_sem.at[0])
    own_m = pltpu.make_async_copy(meta_v, meta, local_sem.at[1])
    for lay in lays:
        lay.start()
    own_v.start()
    own_m.start()
    barrier = pltpu.get_barrier_semaphore()
    for device in (across, beside, twin):
        pl.semaphore_signal(barrier, inc=1, device_id=device, device_id_type=MESH)
    pl.when(has_up)(lambda: pl.semaphore_signal(barrier, inc=1, device_id=up, device_id_type=MESH))
    pl.when(has_down)(lambda: pl.semaphore_signal(barrier, inc=1, device_id=down, device_id_type=MESH))
    for lay in lays:
        lay.wait()
    pl.semaphore_wait(barrier, 3 + has_up.astype(jnp.int32) + has_down.astype(jnp.int32))

    vy = copy(v, v_other, one_send.at[0], one_recv.at[0], beside)
    my = copy(meta_v, meta_in, one_send.at[1], one_recv.at[1], beside)
    for qz, qx in zip(even + odd, odd + even):
        for move in onward(0, None):
            guarded(move[2], lambda move=move: z_copy(0, 0, qz, move).start())
        x_copy(0, qx).start()
    my.start()
    vy.start()

    def relay(k, kind, q):
        for b, zp, valid, way in shards(k):
            def run(b=b, way=way):
                z_wait(b, kind, q)
                for move in onward(b, way):
                    guarded(move[2], lambda move=move: z_copy(b, kind, q, move).start())
                if kind == 0:
                    if q in even:
                        x_copy(b, q).start()
                    else:
                        pl.when(jnp.logical_not(is_end(k, way)))(lambda: x_copy(b, q).start())

            guarded(valid if kind == 0 else both(valid, is_end(k, way)), run)

    def relay_own(q):
        x_wait(0, q)

        def run():
            for move in onward(0, None):
                guarded(move[2], lambda move=move: z_copy(0, 1, q, move).start())

        pl.when(at_end)(run)

    def span(h):
        return pl.ds(2 * h * chunk, 2 * chunk)

    def core_copy(zp, strip, h):
        return copy(part.at[zp, strip, :, span(h)], core_in.at[zp % half, strip, :, span(h)],
                    core_send.at[zp, strip, h], core_recv.at[zp, strip, h], twin)

    def target(zp, h):
        return out.at[zp % half * 2 + y, :, span(h)]

    def y_copy(zp, h):
        return copy(y_out.at[zp % half, :, span(h)], target(zp, h), y_send.at[zp, h], y_recv.at[zp, h], beside)

    def own_copy(zp, h):
        return pltpu.make_async_copy(own_out.at[zp % half, :, span(h)], target(zp, h), own_sem.at[zp, h])

    def mine(zp):
        return zp // half == core

    strips = ((v_other, meta_other), (v_own, meta))

    def products(b, zp, h):
        def slot(s, carry):
            for strip, (stored, info) in enumerate(strips):
                at_row = info[1, s]
                left = jnp.concatenate([bufs[b][q][side, at_row] for side in (0, 1) for q in (2 * h, 2 * h + 1)], axis=0)
                new = jnp.dot(left, stored[info[0, s]], preferred_element_type=jnp.float32)
                runs[strip, s + 1] = new + runs[strip, s] * info[2, s].astype(jnp.float32)
            return carry

        lax.fori_loop(0, slots, slot, 0, unroll=8)
        for strip, (stored, info) in enumerate(strips):
            for c in range(col_blocks):
                value = runs[strip, info[3, c] + 1] * info[4, c].astype(jnp.float32)
                part[zp, strip, :, span(h), c * size:(c + 1) * size] = value.reshape(2, 2 * chunk, size)
            pl.when(jnp.logical_not(mine(zp)))(lambda: core_copy(zp, strip, h).start())

    def compute(k, h):
        for b, zp, valid, way in shards(k):
            def run(b=b, zp=zp, way=way):
                x_wait(b, 2 * h)
                if k == depth - 1:
                    z_wait(b, 1, 2 * h + 1)
                elif k > 0:
                    pl.when(jnp.logical_not(is_end(k, way)))(lambda: x_wait(b, 2 * h + 1))
                products(b, zp, h)

            guarded(valid, run)

    def finish(k, h):
        for b, zp, valid, way in shards(k):
            def run(zp=zp):
                core_copy(zp, 0, h).wait_recv()
                y_out[zp % half, :, span(h)] = part[zp, 0, :, span(h)] + core_in[zp % half, 0, :, span(h)]
                y_copy(zp, h).start()
                core_copy(zp, 1, h).wait_recv()
                own_out[zp % half, :, span(h)] = part[zp, 1, :, span(h)] + core_in[zp % half, 1, :, span(h)]
                own_copy(zp, h).start()

            guarded(both(valid, mine(zp)), run)

    for strip in (0, 1):
        runs[strip, 0] = jnp.zeros(runs.shape[2:], jnp.float32)
    for q in even:
        relay(1, 0, q)
    for q in odd:
        relay_own(q)
    for q in odd:
        relay(1, 0, q)
    for k in range(2, depth - 1):
        for qk, ql in zip(even, odd):
            relay(k, 0, qk)
            relay(k - 1, 1, ql)
        for q in odd:
            relay(k, 0, q)
    own_v.wait()
    own_m.wait()
    my.wait_recv()
    into = pltpu.make_async_copy(meta_in, meta_other, local_sem.at[2])
    into.start()
    into.wait()
    vy.wait_recv()
    compute(0, 0)
    compute(0, 1)
    finish(0, 0)
    for q in odd:
        relay(depth - 2, 1, q)
    waiting = [(0, 1)]
    for k in range(1, depth):
        if k == depth - 2:
            for q in even + odd:
                relay(depth - 1, 0, q)
        for h in range(halves):
            compute(k, h)
            for todo in waiting:
                finish(*todo)
            waiting = [(k, h)]
    for todo in waiting:
        finish(*todo)

    vy.wait_send()
    my.wait_send()
    for k in range(depth):
        for b, zp, valid, way in shards(k):
            def run(b=b, zp=zp, way=way):
                for move in onward(b, way):
                    guarded(move[2], lambda move=move: [z_copy(b, 0, q, move).wait_send() for q in range(pieces)] and None)
                    guarded(both(is_end(k, way), move[2]), lambda move=move: [z_copy(b, 1, q, move).wait_send() for q in odd] and None)
                for q in even:
                    x_copy(b, q).wait_send()
                guarded(None if k == 0 else jnp.logical_not(is_end(k, way)), lambda: [x_copy(b, q).wait_send() for q in odd] and None)
                other = jnp.logical_not(mine(zp))
                pl.when(other)(lambda: [core_copy(zp, j, h).wait_send() for j in (0, 1) for h in range(halves)] and None)
                pl.when(mine(zp))(lambda: [(y_copy(zp, h).wait(), own_copy(zp, h).wait()) for h in range(halves)] and None)

            guarded(valid, run)


def slot_table(places, count, col_blocks):
    total = places.shape[0]
    ids = jnp.arange(total, dtype=jnp.int32)
    cols = jnp.where(ids < count, places % col_blocks, col_blocks)
    key = cols * total + ids
    rank = jnp.sum((key[None, :] < key[:, None]).astype(jnp.int32), axis=1)
    hit = (rank[:, None] == ids[None, :]).astype(jnp.int32)
    order = jnp.sum(hit * ids[:, None], axis=0)
    row = jnp.sum(hit * (places // col_blocks)[:, None], axis=0)
    col = jnp.sum(hit * cols[:, None], axis=0)
    before = jnp.sum((rank[:, None] + 1 == ids[None, :]).astype(jnp.int32) * (cols + 1)[:, None], axis=0) - 1
    same = (col == before).astype(jnp.int32)
    each = jnp.arange(col_blocks, dtype=jnp.int32)
    last = jnp.sum((cols[None, :] <= each[:, None]).astype(jnp.int32), axis=1) - 1
    some = jnp.sum((cols[None, :] == each[:, None]).astype(jnp.int32), axis=1)
    lanes = -(-max(total, col_blocks) // 128) * 128

    def wide(a):
        return jnp.pad(a, (0, lanes - a.shape[0]))

    zero = jnp.zeros((lanes,), jnp.int32)
    return jnp.stack([wide(order), wide(row), wide(same), wide(jnp.maximum(last, 0)), wide(jnp.minimum(some, 1)), zero, zero, zero])


def ring_shards(width, wide_size, t_amps, v_blocks, block_pos, block_count):
    rows, columns = t_amps.shape
    slots, size = v_blocks.shape[2], v_blocks.shape[3]
    depth = wide_size // 4
    half, buffers = depth // 2, 2 * depth - 1
    strip = width // wide_size
    chunk = rows // PIECES
    meta = slot_table(block_pos[0, 0], block_count[0, 0], strip // size)
    by_piece = jnp.transpose(t_amps.reshape(PIECES, chunk, columns // size, size), (0, 2, 1, 3))
    bf16, f32, i32 = jnp.bfloat16, jnp.float32, jnp.int32
    dma = pltpu.SemaphoreType.DMA
    out = pl.pallas_call(
        functools.partial(ladder_kernel, depth),
        out_shape=jax.ShapeDtypeStruct((half * 2, 2, rows, strip), f32),
        in_specs=[
            pl.BlockSpec(memory_space=pltpu.HBM),
            pl.BlockSpec(memory_space=pltpu.HBM),
            pl.BlockSpec(memory_space=pltpu.VMEM),
        ],
        out_specs=pl.BlockSpec(memory_space=pl.ANY),
        scratch_shapes=[pltpu.VMEM((2, columns // size, chunk, size), bf16)] * (buffers * PIECES) + [
            pltpu.VMEM((slots, size, size), bf16),
            pltpu.VMEM((slots, size, size), bf16),
            pltpu.VMEM(meta.shape, i32),
            pltpu.SMEM(meta.shape, i32),
            pltpu.SMEM(meta.shape, i32),
            pltpu.VMEM((2, slots + 1, 4 * chunk, size), f32),
            pltpu.VMEM((depth, 2, 2, rows, strip), f32),
            pltpu.VMEM((half, 2, 2, rows, strip), f32),
            pltpu.VMEM((half, 2, rows, strip), f32),
            pltpu.VMEM((half, 2, rows, strip), f32),
            dma((PIECES,)),
            dma((3,)),
            dma((2, buffers, 2, PIECES)), dma((buffers, 2, PIECES)),
            dma((buffers, PIECES)), dma((buffers, PIECES)),
            dma((2,)), dma((2,)),
            dma((depth, 2, PIECES // 2)), dma((depth, 2, PIECES // 2)),
            dma((depth, PIECES // 2)), dma((depth, PIECES // 2)),
            dma((depth, PIECES // 2)),
        ],
        compiler_params=pltpu.CompilerParams(
            collective_id=0, has_side_effects=True, vmem_limit_bytes=36 * 1024 * 1024
        ),
    )(by_piece, v_blocks, meta)
    return out.reshape(half * 4 * rows, strip)


def solution(mesh):
    in_specs = (
        P("wide", "narrow"),
        P("narrow", "wide", None, None, None),
        P("narrow", "wide", None),
        P("narrow", "wide"),
    )
    out_specs = P("narrow", "wide")
    wide_size, narrow_size = mesh.shape["wide"], mesh.shape["narrow"]

    def program(t_amps, v_blocks, block_pos, block_count):
        width = t_amps.shape[1]
        if narrow_size == 2 and wide_size >= 16 and wide_size % 8 == 0:
            body = functools.partial(ring_shards, width, wide_size)
        else:
            body = functools.partial(dense_shards, width)
        run = jax.shard_map(body, mesh=mesh, in_specs=in_specs, out_specs=out_specs, check_vma=False)
        return run(t_amps, v_blocks, block_pos, block_count)

    return program
```

```python
import functools

import jax
import jax.numpy as jnp
from jax import lax
from jax.experimental import pallas as pl
from jax.experimental.pallas import tpu as pltpu
from jax.sharding import PartitionSpec as P

MESH = pl.DeviceIdType.MESH
PIECES = 4


def dense_shards(width, t_amps, v_blocks, block_pos, block_count):
    stored = v_blocks[0, 0]
    places = block_pos[0, 0]
    slot_count = block_count[0, 0]
    block_size = stored.shape[1]
    slot_total = stored.shape[0]
    row_blocks = t_amps.shape[1] // block_size
    col_blocks = width // (lax.axis_size("wide") * block_size)
    live_mask = (jnp.arange(slot_total, dtype=jnp.int32) < slot_count).astype(jnp.bfloat16)
    masked = stored * live_mask[:, None, None]
    dense_tile = jnp.zeros((row_blocks * col_blocks, block_size, block_size), jnp.bfloat16)
    dense_tile = dense_tile.at[places].add(masked)
    dense_tile = dense_tile.reshape(row_blocks, col_blocks, block_size, block_size)
    dense_tile = jnp.transpose(dense_tile, (0, 2, 1, 3)).reshape(row_blocks * block_size, col_blocks * block_size)
    gathered = lax.all_gather(t_amps, "wide", axis=0, tiled=True)
    partial_sum = jnp.dot(gathered, dense_tile, preferred_element_type=jnp.float32)
    return lax.psum_scatter(partial_sum, "narrow", scatter_dimension=0, tiled=True)


def ladder_kernel(depth, t, v_tile, meta_v, out, *scratch):
    held = scratch[: (2 * depth - 1) * PIECES]
    bufs = [held[b * PIECES:(b + 1) * PIECES] for b in range(2 * depth - 1)]
    (v_own, v_other, meta_in, meta, meta_other, runs, part, core_in, y_out, own_out,
     lay_sem, local_sem, z_send, z_recv, x_send, x_recv, one_send, one_recv, core_send, core_recv, y_send, y_recv,
     own_sem) = scratch[(2 * depth - 1) * PIECES:]
    wide, core = lax.axis_index("wide"), lax.axis_index("narrow")
    z, y, x = wide // 4, (wide // 2) % 2, wide % 2
    up, down = (wide + 4, core), (wide - 4, core)
    across = (wide + 1 - 2 * x, core)
    beside = (wide + 2 - 4 * y, core)
    twin = (wide, 1 - core)
    half = depth // 2
    pieces, row_blocks, chunk, unused = t.shape
    v = v_tile.at[0, 0]
    slots, size = v.shape[0], v.shape[1]
    col_blocks = out.shape[-1] // size
    has_up, has_down = z < depth - 1, z > 0
    at_end = jnp.logical_or(z == 0, z == depth - 1)
    first = row_blocks // 2
    second_cols = pl.ds(first, row_blocks - first)

    def copy(src, dst, send, recv, device):
        return pltpu.make_async_remote_copy(
            src_ref=src, dst_ref=dst, send_sem=send, recv_sem=recv, device_id=device, device_id_type=MESH
        )

    def guarded(cond, fn):
        if cond is None:
            fn()
        else:
            pl.when(cond)(fn)

    def both(a, b):
        return b if a is None else a if b is None else jnp.logical_and(a, b)

    def shards(k):
        if k == 0:
            return [(0, z, None, None)]
        return [(k, z - k, z >= k, 0), (depth - 1 + k, z + k, z + k < depth, 1)]

    def is_end(k, way):
        return at_end if k == 0 else (z == k) if way == 0 else (z + k == depth - 1)

    def onward(b, way):
        ups = [] if way == 1 or b == depth - 1 else [(0, up, has_up, b + 1)]
        downs = [] if way == 0 or b == 2 * depth - 2 else [(1, down, has_down, depth if b == 0 else b + 1)]
        return ups + downs

    def z_ref(b, kind, q):
        return bufs[b][q].at[x] if kind == 0 else bufs[b][q].at[1 - x, second_cols]

    def z_copy(b, kind, q, move):
        direction, device, unused, landing = move
        return copy(z_ref(b, kind, q), z_ref(landing, kind, q), z_send.at[direction, b, kind, q], z_recv.at[landing, kind, q], device)

    def x_copy(b, q, cols, side):
        ref = bufs[b][q].at[side, pl.ds(0, cols)]
        return copy(ref, ref, x_send.at[b, q], x_recv.at[b, q], across)

    def z_wait(b, kind, q):
        ref = z_ref(b, kind, q)
        copy(ref, ref, z_send.at[0, b, kind, q], z_recv.at[b, kind, q], up).wait_recv()

    def crossing(k, way, fn):
        if k == 0:
            fn(row_blocks)
        elif k == depth - 1:
            fn(first)
        else:
            pl.when(is_end(k, way))(lambda: fn(first))
            pl.when(jnp.logical_not(is_end(k, way)))(lambda: fn(row_blocks))

    def x_start(k, b, way, q):
        crossing(k, way, lambda cols: x_copy(b, q, cols, x).start())

    def x_wait(k, b, way, q):
        crossing(k, way, lambda cols: x_copy(b, q, cols, 1 - x).wait_recv())

    lays = [pltpu.make_async_copy(t.at[q], bufs[0][q].at[x], lay_sem.at[q]) for q in range(pieces)]
    own_v = pltpu.make_async_copy(v, v_own, local_sem.at[0])
    own_m = pltpu.make_async_copy(meta_v, meta, local_sem.at[1])
    for lay in lays:
        lay.start()
    own_v.start()
    own_m.start()
    barrier = pltpu.get_barrier_semaphore()
    for device in (across, beside, twin):
        pl.semaphore_signal(barrier, inc=1, device_id=device, device_id_type=MESH)
    pl.when(has_up)(lambda: pl.semaphore_signal(barrier, inc=1, device_id=up, device_id_type=MESH))
    pl.when(has_down)(lambda: pl.semaphore_signal(barrier, inc=1, device_id=down, device_id_type=MESH))
    for lay in lays:
        lay.wait()
    pl.semaphore_wait(barrier, 3 + has_up.astype(jnp.int32) + has_down.astype(jnp.int32))

    vy = copy(v, v_other, one_send.at[0], one_recv.at[0], beside)
    my = copy(meta_v, meta_in, one_send.at[1], one_recv.at[1], beside)
    for q in range(pieces):
        for move in onward(0, None):
            guarded(move[2], lambda move=move: z_copy(0, 0, q, move).start())
        x_start(0, 0, None, q)
    my.start()
    vy.start()

    def relay(k, kind, q):
        for b, zp, valid, way in shards(k):
            def run(b=b, way=way):
                z_wait(b, kind, q)
                for move in onward(b, way):
                    guarded(move[2], lambda move=move: z_copy(b, kind, q, move).start())
                if kind == 0:
                    x_start(k, b, way, q)

            guarded(valid if kind == 0 else both(valid, is_end(k, way)), run)

    def relay_own(q):
        x_wait(0, 0, None, q)

        def run():
            for move in onward(0, None):
                guarded(move[2], lambda move=move: z_copy(0, 1, q, move).start())

        pl.when(at_end)(run)

    def groups(k):
        count = 1 if k == depth - 1 else 2
        return [(q, count) for q in range(0, pieces, count)]

    def span(g):
        return pl.ds(g[0] * chunk, g[1] * chunk)

    def core_copy(zp, strip, g):
        return copy(part.at[zp, strip, :, span(g)], core_in.at[zp % half, strip, :, span(g)],
                    core_send.at[zp, strip, g[0]], core_recv.at[zp, strip, g[0]], twin)

    def target(zp, g):
        return out.at[zp % half * 2 + y, :, span(g)]

    def y_copy(zp, g):
        return copy(y_out.at[zp % half, :, span(g)], target(zp, g), y_send.at[zp, g[0]], y_recv.at[zp, g[0]], beside)

    def own_copy(zp, g):
        return pltpu.make_async_copy(own_out.at[zp % half, :, span(g)], target(zp, g), own_sem.at[zp, g[0]])

    def mine(zp):
        return zp // half == core

    tables = ((v_other, meta_other), (v_own, meta))

    def products(b, zp, g, strips, unroll):
        lines = 2 * g[1] * chunk

        def slot(s, carry):
            for strip in strips:
                stored, info = tables[strip]
                at_row = info[1, s]
                left = jnp.concatenate([bufs[b][q][side, at_row] for side in (0, 1) for q in range(g[0], g[0] + g[1])], axis=0)
                new = jnp.dot(left, stored[info[0, s]], preferred_element_type=jnp.float32)
                runs[strip, s + 1, :lines] = new + runs[strip, s, :lines] * info[2, s].astype(jnp.float32)
            return carry

        lax.fori_loop(0, slots, slot, 0, unroll=unroll)
        for strip in strips:
            info = tables[strip][1]
            for c in range(col_blocks):
                value = runs[strip, info[3, c] + 1, :lines] * info[4, c].astype(jnp.float32)
                part[zp, strip, :, span(g), c * size:(c + 1) * size] = value.reshape(2, g[1] * chunk, size)
            pl.when(jnp.logical_not(mine(zp)))(lambda: core_copy(zp, strip, g).start())

    def compute(k, g, ahead=None):
        for b, zp, valid, way in shards(k):
            def run(b=b, zp=zp, way=way):
                for q in range(g[0], g[0] + g[1]):
                    if k > 0:
                        x_wait(k, b, way, q)
                    if k == depth - 1:
                        z_wait(b, 1, q)
                if ahead is None:
                    products(b, zp, g, (0, 1), 16)
                else:
                    products(b, zp, g, (0,), 32)
                    finish(k, ahead, b)
                    products(b, zp, g, (1,), 32)

            guarded(valid, run)

    def finish(k, g, only=None):
        for b, zp, valid, way in shards(k):
            def run(zp=zp):
                core_copy(zp, 0, g).wait_recv()
                y_out[zp % half, :, span(g)] = part[zp, 0, :, span(g)] + core_in[zp % half, 0, :, span(g)]
                y_copy(zp, g).start()
                core_copy(zp, 1, g).wait_recv()
                own_out[zp % half, :, span(g)] = part[zp, 1, :, span(g)] + core_in[zp % half, 1, :, span(g)]
                own_copy(zp, g).start()

            if only is None:
                guarded(both(valid, mine(zp)), run)
            elif only == b:
                pl.when(mine(zp))(run)

    for strip in (0, 1):
        runs[strip, 0] = jnp.zeros(runs.shape[2:], jnp.float32)
    for q in range(pieces):
        relay(1, 0, q)
        relay_own(q)
    for k in range(2, depth - 1):
        for q in range(pieces):
            relay(k - 1, 1, q)
            relay(k, 0, q)
    own_v.wait()
    own_m.wait()
    my.wait_recv()
    into = pltpu.make_async_copy(meta_in, meta_other, local_sem.at[2])
    into.start()
    into.wait()
    vy.wait_recv()
    for g in groups(0):
        compute(0, g)
    finish(0, groups(0)[0])
    compute(1, groups(1)[0])
    finish(0, groups(0)[1])
    for q in range(pieces):
        relay(depth - 2, 1, q)
    compute(1, groups(1)[1])
    finish(1, groups(1)[0])
    finish(1, groups(1)[1])
    for k in range(2, depth - 1):
        for n, g in enumerate(groups(k)):
            if k == depth - 2:
                for q in range(2 * n, 2 * n + 2):
                    relay(depth - 1, 0, q)
            compute(k, g)
            finish(k, g)
    ahead = None
    for g in groups(depth - 1):
        last = g[0] == pieces - 1
        compute(depth - 1, g, ahead if last else None)
        if ahead is not None and not last:
            finish(depth - 1, ahead)
        ahead = g
    finish(depth - 1, ahead)

    vy.wait_send()
    my.wait_send()
    for k in range(depth):
        for b, zp, valid, way in shards(k):
            def run(b=b, zp=zp, way=way):
                for move in onward(b, way):
                    guarded(move[2], lambda move=move: [z_copy(b, 0, q, move).wait_send() for q in range(pieces)] and None)
                    guarded(both(is_end(k, way), move[2]), lambda move=move: [z_copy(b, 1, q, move).wait_send() for q in range(pieces)] and None)
                crossing(k, way, lambda cols: [x_copy(b, q, cols, x).wait_send() for q in range(pieces)] and None)
                other = jnp.logical_not(mine(zp))
                pl.when(other)(lambda: [core_copy(zp, j, g).wait_send() for j in (0, 1) for g in groups(k)] and None)
                pl.when(mine(zp))(lambda: [(y_copy(zp, g).wait(), own_copy(zp, g).wait()) for g in groups(k)] and None)

            guarded(valid, run)


def slot_table(places, count, col_blocks):
    total = places.shape[0]
    ids = jnp.arange(total, dtype=jnp.int32)
    cols = jnp.where(ids < count, places % col_blocks, col_blocks)
    key = cols * total + ids
    rank = jnp.sum((key[None, :] < key[:, None]).astype(jnp.int32), axis=1)
    hit = (rank[:, None] == ids[None, :]).astype(jnp.int32)
    order = jnp.sum(hit * ids[:, None], axis=0)
    row = jnp.sum(hit * (places // col_blocks)[:, None], axis=0)
    col = jnp.sum(hit * cols[:, None], axis=0)
    before = jnp.sum((rank[:, None] + 1 == ids[None, :]).astype(jnp.int32) * (cols + 1)[:, None], axis=0) - 1
    same = (col == before).astype(jnp.int32)
    each = jnp.arange(col_blocks, dtype=jnp.int32)
    last = jnp.sum((cols[None, :] <= each[:, None]).astype(jnp.int32), axis=1) - 1
    some = jnp.sum((cols[None, :] == each[:, None]).astype(jnp.int32), axis=1)
    lanes = -(-max(total, col_blocks) // 128) * 128

    def wide(a):
        return jnp.pad(a, (0, lanes - a.shape[0]))

    zero = jnp.zeros((lanes,), jnp.int32)
    return jnp.stack([wide(order), wide(row), wide(same), wide(jnp.maximum(last, 0)), wide(jnp.minimum(some, 1)), zero, zero, zero])


def ring_shards(width, wide_size, t_amps, v_blocks, block_pos, block_count):
    rows, columns = t_amps.shape
    slots, size = v_blocks.shape[2], v_blocks.shape[3]
    depth = wide_size // 4
    half, buffers = depth // 2, 2 * depth - 1
    strip = width // wide_size
    chunk = rows // PIECES
    meta = slot_table(block_pos[0, 0], block_count[0, 0], strip // size)
    by_piece = jnp.transpose(t_amps.reshape(PIECES, chunk, columns // size, size), (0, 2, 1, 3))
    bf16, f32, i32 = jnp.bfloat16, jnp.float32, jnp.int32
    dma = pltpu.SemaphoreType.DMA
    out = pl.pallas_call(
        functools.partial(ladder_kernel, depth),
        out_shape=jax.ShapeDtypeStruct((half * 2, 2, rows, strip), f32),
        in_specs=[
            pl.BlockSpec(memory_space=pltpu.HBM),
            pl.BlockSpec(memory_space=pltpu.HBM),
            pl.BlockSpec(memory_space=pltpu.VMEM),
        ],
        out_specs=pl.BlockSpec(memory_space=pl.ANY),
        scratch_shapes=[pltpu.VMEM((2, columns // size, chunk, size), bf16)] * (buffers * PIECES) + [
            pltpu.VMEM((slots, size, size), bf16),
            pltpu.VMEM((slots, size, size), bf16),
            pltpu.VMEM(meta.shape, i32),
            pltpu.SMEM(meta.shape, i32),
            pltpu.SMEM(meta.shape, i32),
            pltpu.VMEM((2, slots + 1, 4 * chunk, size), f32),
            pltpu.VMEM((depth, 2, 2, rows, strip), f32),
            pltpu.VMEM((half, 2, 2, rows, strip), f32),
            pltpu.VMEM((half, 2, rows, strip), f32),
            pltpu.VMEM((half, 2, rows, strip), f32),
            dma((PIECES,)),
            dma((3,)),
            dma((2, buffers, 2, PIECES)), dma((buffers, 2, PIECES)),
            dma((buffers, PIECES)), dma((buffers, PIECES)),
            dma((2,)), dma((2,)),
            dma((depth, 2, PIECES)), dma((depth, 2, PIECES)),
            dma((depth, PIECES)), dma((depth, PIECES)),
            dma((depth, PIECES)),
        ],
        compiler_params=pltpu.CompilerParams(
            collective_id=0, has_side_effects=True, vmem_limit_bytes=40 * 1024 * 1024
        ),
    )(pltpu.with_memory_space_constraint(by_piece, pltpu.HBM), pltpu.with_memory_space_constraint(v_blocks, pltpu.HBM), meta)
    return out.reshape(half * 4 * rows, strip)


def solution(mesh):
    in_specs = (
        P("wide", "narrow"),
        P("narrow", "wide", None, None, None),
        P("narrow", "wide", None),
        P("narrow", "wide"),
    )
    out_specs = P("narrow", "wide")
    wide_size, narrow_size = mesh.shape["wide"], mesh.shape["narrow"]

    def program(t_amps, v_blocks, block_pos, block_count):
        width = t_amps.shape[1]
        if narrow_size == 2 and wide_size >= 16 and wide_size % 8 == 0:
            body = functools.partial(ring_shards, width, wide_size)
        else:
            body = functools.partial(dense_shards, width)
        run = jax.shard_map(body, mesh=mesh, in_specs=in_specs, out_specs=out_specs, check_vma=False)
        return run(t_amps, v_blocks, block_pos, block_count)

    return program
```

```python
import functools

import jax
import jax.numpy as jnp
from jax import lax
from jax.experimental import pallas as pl
from jax.experimental.pallas import tpu as pltpu
from jax.sharding import PartitionSpec as P

MESH = pl.DeviceIdType.MESH
PIECES = 4


def dense_shards(width, t_amps, v_blocks, block_pos, block_count):
    stored = v_blocks[0, 0]
    places = block_pos[0, 0]
    slot_count = block_count[0, 0]
    block_size = stored.shape[1]
    slot_total = stored.shape[0]
    row_blocks = t_amps.shape[1] // block_size
    col_blocks = width // (lax.axis_size("wide") * block_size)
    live_mask = (jnp.arange(slot_total, dtype=jnp.int32) < slot_count).astype(jnp.bfloat16)
    masked = stored * live_mask[:, None, None]
    dense_tile = jnp.zeros((row_blocks * col_blocks, block_size, block_size), jnp.bfloat16)
    dense_tile = dense_tile.at[places].add(masked)
    dense_tile = dense_tile.reshape(row_blocks, col_blocks, block_size, block_size)
    dense_tile = jnp.transpose(dense_tile, (0, 2, 1, 3)).reshape(row_blocks * block_size, col_blocks * block_size)
    gathered = lax.all_gather(t_amps, "wide", axis=0, tiled=True)
    partial_sum = jnp.dot(gathered, dense_tile, preferred_element_type=jnp.float32)
    return lax.psum_scatter(partial_sum, "narrow", scatter_dimension=0, tiled=True)


def ladder_kernel(depth, t, v_tile, pos, count, out, *scratch):
    total = (2 * depth - 1) * PIECES * 2
    bufs = [[scratch[2 * (b * PIECES + q):2 * (b * PIECES + q) + 2] for q in range(PIECES)] for b in range(2 * depth - 1)]
    (v_own, v_other, pos_own, count_own, pos_other, count_other, made, info_own, info_other, runs, part, core_in, y_out, own_out,
     lay_sem, local_sem, z_send, z_recv, x_send, x_recv, one_send, one_recv, core_send, core_recv, y_send, y_recv,
     own_sem) = scratch[total:]
    wide, core = lax.axis_index("wide"), lax.axis_index("narrow")
    z, y, x = wide // 4, (wide // 2) % 2, wide % 2
    up, down = (wide + 4, core), (wide - 4, core)
    across = (wide + 1 - 2 * x, core)
    beside = (wide + 2 - 4 * y, core)
    twin = (wide, 1 - core)
    half = depth // 2
    pieces, row_blocks, chunk, unused = t.shape
    v = v_tile.at[0, 0]
    slots, size = v.shape[0], v.shape[1]
    col_blocks = out.shape[-1] // size
    has_up, has_down = z < depth - 1, z > 0
    at_end = jnp.logical_or(z == 0, z == depth - 1)
    first = row_blocks // 2
    second_cols = pl.ds(first, row_blocks - first)

    def copy(src, dst, send, recv, device):
        return pltpu.make_async_remote_copy(
            src_ref=src, dst_ref=dst, send_sem=send, recv_sem=recv, device_id=device, device_id_type=MESH
        )

    def guarded(cond, fn):
        if cond is None:
            fn()
        else:
            pl.when(cond)(fn)

    def both(a, b):
        return b if a is None else a if b is None else jnp.logical_and(a, b)

    def shards(k):
        if k == 0:
            return [(0, z, None, None)]
        return [(k, z - k, z >= k, 0), (depth - 1 + k, z + k, z + k < depth, 1)]

    def is_end(k, way):
        return at_end if k == 0 else (z == k) if way == 0 else (z + k == depth - 1)

    def onward(b, way):
        ups = [] if way == 1 or b == depth - 1 else [(0, up, has_up, b + 1)]
        downs = [] if way == 0 or b == 2 * depth - 2 else [(1, down, has_down, depth if b == 0 else b + 1)]
        return ups + downs

    def z_ref(b, kind, q):
        return bufs[b][q][0] if kind == 0 else bufs[b][q][1].at[second_cols]

    def z_copy(b, kind, q, move):
        direction, device, unused, landing = move
        return copy(z_ref(b, kind, q), z_ref(landing, kind, q), z_send.at[direction, b, kind, q], z_recv.at[landing, kind, q], device)

    def x_copy(b, q, cols):
        mine_side, other_side = (ref.at[pl.ds(0, cols)] for ref in bufs[b][q])
        return copy(mine_side, other_side, x_send.at[b, q], x_recv.at[b, q], across)

    def z_wait(b, kind, q):
        ref = z_ref(b, kind, q)
        copy(ref, ref, z_send.at[0, b, kind, q], z_recv.at[b, kind, q], up).wait_recv()

    def crossing(k, way, fn):
        if k == 0:
            fn(row_blocks)
        elif k == depth - 1:
            fn(first)
        else:
            pl.when(is_end(k, way))(lambda: fn(first))
            pl.when(jnp.logical_not(is_end(k, way)))(lambda: fn(row_blocks))

    def x_start(k, b, way, q):
        crossing(k, way, lambda cols: x_copy(b, q, cols).start())

    def x_wait(k, b, way, q):
        crossing(k, way, lambda cols: x_copy(b, q, cols).wait_recv())

    lays = [pltpu.make_async_copy(t.at[q], bufs[0][q][0], lay_sem.at[q]) for q in range(pieces)]
    own_v = pltpu.make_async_copy(v, v_own, local_sem.at[0])
    own_p = pltpu.make_async_copy(pos, pos_own, local_sem.at[1])
    own_c = pltpu.make_async_copy(count, count_own, local_sem.at[2])
    for lay in lays:
        lay.start()
    own_v.start()
    own_p.start()
    own_c.start()
    barrier = pltpu.get_barrier_semaphore()
    for device in (across, beside, twin):
        pl.semaphore_signal(barrier, inc=1, device_id=device, device_id_type=MESH)
    pl.when(has_up)(lambda: pl.semaphore_signal(barrier, inc=1, device_id=up, device_id_type=MESH))
    pl.when(has_down)(lambda: pl.semaphore_signal(barrier, inc=1, device_id=down, device_id_type=MESH))
    for lay in lays:
        lay.wait()
    pl.semaphore_wait(barrier, 3 + has_up.astype(jnp.int32) + has_down.astype(jnp.int32))

    vy = copy(v, v_other, one_send.at[0], one_recv.at[0], beside)
    py = copy(pos, pos_other, one_send.at[1], one_recv.at[1], beside)
    cy = copy(count, count_other, one_send.at[2], one_recv.at[2], beside)
    for q in range(pieces):
        for move in onward(0, None):
            guarded(move[2], lambda move=move: z_copy(0, 0, q, move).start())
        x_start(0, 0, None, q)
    py.start()
    cy.start()
    vy.start()

    def relay(k, kind, q):
        for b, zp, valid, way in shards(k):
            def run(b=b, way=way):
                z_wait(b, kind, q)
                for move in onward(b, way):
                    guarded(move[2], lambda move=move: z_copy(b, kind, q, move).start())
                if kind == 0:
                    x_start(k, b, way, q)

            guarded(valid if kind == 0 else both(valid, is_end(k, way)), run)

    def relay_own(q):
        x_wait(0, 0, None, q)

        def run():
            for move in onward(0, None):
                guarded(move[2], lambda move=move: z_copy(0, 1, q, move).start())

        pl.when(at_end)(run)

    def steps(k):
        if k == depth - 1:
            tail = [(1 - x, (1,), (0, 1))] + [(1 - x, (1,), (q,)) for q in range(2, pieces)]
            return [(x, (0,), tuple(range(pieces)))] + tail
        return [(pl.ds(0, 2), (0, 1), (q, q + 1)) for q in range(0, pieces, 2)]

    def span(k, n):
        sides, unused, qs = steps(k)[n]
        return sides, pl.ds(qs[0] * chunk, len(qs) * chunk)

    def core_copy(zp, strip, k, n):
        return copy(part.at[zp, strip, *span(k, n)], core_in.at[zp % half, strip, *span(k, n)],
                    core_send.at[zp, strip, n], core_recv.at[zp, strip, n], twin)

    def target(zp, k, n):
        return out.at[zp % half * 2 + y, *span(k, n)]

    def y_copy(zp, k, n):
        return copy(y_out.at[zp % half, *span(k, n)], target(zp, k, n), y_send.at[zp, n], y_recv.at[zp, n], beside)

    def own_copy(zp, k, n):
        return pltpu.make_async_copy(own_out.at[zp % half, *span(k, n)], target(zp, k, n), own_sem.at[zp, n])

    def mine(zp):
        return zp // half == core

    def chain(places, live, strip):
        place = places[0]
        shift = (col_blocks - 1).bit_length()
        row = place >> shift if col_blocks == 1 << shift else place // col_blocks
        along = jnp.broadcast_to(place - row * col_blocks, (slots, slots))
        down = along.T
        earlier = lax.broadcasted_iota(jnp.int32, (slots, slots), 0)
        at = lax.broadcasted_iota(jnp.int32, (slots, slots), 1)
        known = jnp.where(earlier < live[...], earlier + 1, 0)
        before = jnp.max(jnp.where(jnp.logical_and(down == along, earlier < at), known, 0), axis=0, keepdims=True)
        last = jnp.max(jnp.where(down == at, known, 0), axis=0, keepdims=True)
        for i, line in enumerate((row, before, last)):
            made[strip, i:i + 1, :slots] = line

    tables = ((v_other, info_other), (v_own, info_own))

    def products(b, zp, k, n, strips, unroll):
        unused, sides, qs = steps(k)[n]
        lines = len(sides) * len(qs) * chunk

        def slot(s, carry):
            for strip in strips:
                stored, info = tables[strip]
                at_row = info[0, s]
                left = jnp.concatenate([bufs[b][q][side][at_row] for side in sides for q in qs], axis=0)
                new = jnp.dot(left, stored[s], preferred_element_type=jnp.float32)
                runs[strip, s + 1, :lines] = new + runs[strip, info[1, s], :lines]
            return carry

        lax.fori_loop(0, slots, slot, 0, unroll=unroll)
        for strip in strips:
            info = tables[strip][1]
            for c in range(col_blocks):
                value = runs[strip, info[2, c], :lines]
                for i, side in enumerate(sides):
                    part[zp, strip, x if side == 0 else 1 - x, span(k, n)[1], c * size:(c + 1) * size] = (
                        value[i * len(qs) * chunk:(i + 1) * len(qs) * chunk])
            pl.when(jnp.logical_not(mine(zp)))(lambda: core_copy(zp, strip, k, n).start())

    def compute(k, n, ahead=None):
        for b, zp, valid, way in shards(k):
            def run(b=b, zp=zp, way=way):
                for q in steps(k)[n][2]:
                    if 0 < k < depth - 1 or n > 0 and k > 0:
                        x_wait(k, b, way, q)
                    if n > 0 and k == depth - 1:
                        z_wait(b, 1, q)
                if ahead is None:
                    products(b, zp, k, n, (0, 1), 16)
                else:
                    products(b, zp, k, n, (0,), 32)
                    finish(k, ahead, b)
                    products(b, zp, k, n, (1,), 32)

            guarded(valid, run)

    def finish(k, n, only=None):
        for b, zp, valid, way in shards(k):
            def run(zp=zp):
                core_copy(zp, 0, k, n).wait_recv()
                y_out[zp % half, *span(k, n)] = part[zp, 0, *span(k, n)] + core_in[zp % half, 0, *span(k, n)]
                y_copy(zp, k, n).start()
                core_copy(zp, 1, k, n).wait_recv()
                own_out[zp % half, *span(k, n)] = part[zp, 1, *span(k, n)] + core_in[zp % half, 1, *span(k, n)]
                own_copy(zp, k, n).start()

            if only is None:
                guarded(both(valid, mine(zp)), run)
            elif only == b:
                pl.when(mine(zp))(run)

    for strip in (0, 1):
        runs[strip, 0] = jnp.zeros(runs.shape[2:], jnp.float32)
    for q in range(pieces):
        relay(1, 0, q)
        relay_own(q)
    own_p.wait()
    own_c.wait()
    chain(pos_own, count_own, 1)
    py.wait_recv()
    cy.wait_recv()
    chain(pos_other, count_other, 0)
    for k in range(2, depth - 1):
        for q in range(pieces):
            relay(k - 1, 1, q)
            relay(k, 0, q)
    into = [pltpu.make_async_copy(made.at[strip], tables[strip][1], local_sem.at[3 + strip]) for strip in (0, 1)]
    for each in into:
        each.start()
    for each in into:
        each.wait()
    own_v.wait()
    vy.wait_recv()
    compute(0, 0)
    compute(0, 1)
    finish(0, 0)
    compute(1, 0)
    finish(0, 1)
    for q in range(pieces):
        relay(depth - 2, 1, q)
    compute(1, 1)
    finish(1, 0)
    finish(1, 1)
    for k in range(2, depth - 1):
        for n in range(len(steps(k))):
            if k == depth - 2:
                for q in range(2 * n, 2 * n + 2):
                    relay(depth - 1, 0, q)
            compute(k, n)
            if n == 0:
                finish(k, n)
    compute(depth - 1, 0)
    finish(depth - 2, 1)
    final = len(steps(depth - 1)) - 1
    for n in range(1, final):
        compute(depth - 1, n)
        finish(depth - 1, n - 1)
    compute(depth - 1, final, final - 1)
    finish(depth - 1, final)

    vy.wait_send()
    py.wait_send()
    cy.wait_send()
    for k in range(depth):
        for b, zp, valid, way in shards(k):
            def run(b=b, zp=zp, way=way):
                for move in onward(b, way):
                    guarded(move[2], lambda move=move: [z_copy(b, 0, q, move).wait_send() for q in range(pieces)] and None)
                    guarded(both(is_end(k, way), move[2]), lambda move=move: [z_copy(b, 1, q, move).wait_send() for q in range(pieces)] and None)
                crossing(k, way, lambda cols: [x_copy(b, q, cols).wait_send() for q in range(pieces)] and None)
                other = jnp.logical_not(mine(zp))
                pl.when(other)(lambda: [core_copy(zp, j, k, n).wait_send() for j in (0, 1) for n in range(len(steps(k)))] and None)
                pl.when(mine(zp))(lambda: [(y_copy(zp, k, n).wait(), own_copy(zp, k, n).wait()) for n in range(len(steps(k)))] and None)

            guarded(valid, run)


def ring_shards(width, wide_size, t_amps, v_blocks, block_pos, block_count):
    rows, columns = t_amps.shape
    slots, size = v_blocks.shape[2], v_blocks.shape[3]
    depth = wide_size // 4
    half, buffers = depth // 2, 2 * depth - 1
    strip = width // wide_size
    chunk = rows // PIECES
    lanes = -(-slots // 128) * 128
    by_piece = jnp.transpose(t_amps.reshape(PIECES, chunk, columns // size, size), (0, 2, 1, 3))
    bf16, f32, i32 = jnp.bfloat16, jnp.float32, jnp.int32
    dma = pltpu.SemaphoreType.DMA
    out = pl.pallas_call(
        functools.partial(ladder_kernel, depth),
        out_shape=jax.ShapeDtypeStruct((half * 2, 2, rows, strip), f32),
        in_specs=[
            pl.BlockSpec(memory_space=pltpu.HBM),
            pl.BlockSpec(memory_space=pltpu.HBM),
            pl.BlockSpec(memory_space=pltpu.HBM),
            pl.BlockSpec(memory_space=pltpu.HBM),
        ],
        out_specs=pl.BlockSpec(memory_space=pl.ANY),
        scratch_shapes=[pltpu.VMEM((columns // size, chunk, size), bf16)] * (buffers * PIECES * 2) + [
            pltpu.VMEM((slots, size, size), bf16),
            pltpu.VMEM((slots, size, size), bf16),
            pltpu.VMEM(block_pos.shape, i32), pltpu.VMEM(block_count.shape, i32),
            pltpu.VMEM(block_pos.shape, i32), pltpu.VMEM(block_count.shape, i32),
            pltpu.VMEM((2, 8, lanes), i32),
            pltpu.SMEM((8, lanes), i32), pltpu.SMEM((8, lanes), i32),
            pltpu.VMEM((2, slots + 1, 4 * chunk, size), f32),
            pltpu.VMEM((depth, 2, 2, rows, strip), f32),
            pltpu.VMEM((half, 2, 2, rows, strip), f32),
            pltpu.VMEM((half, 2, rows, strip), f32),
            pltpu.VMEM((half, 2, rows, strip), f32),
            dma((PIECES,)),
            dma((5,)),
            dma((2, buffers, 2, PIECES)), dma((buffers, 2, PIECES)),
            dma((buffers, PIECES)), dma((buffers, PIECES)),
            dma((3,)), dma((3,)),
            dma((depth, 2, PIECES)), dma((depth, 2, PIECES)),
            dma((depth, PIECES)), dma((depth, PIECES)),
            dma((depth, PIECES)),
        ],
        compiler_params=pltpu.CompilerParams(
            collective_id=0, has_side_effects=True, vmem_limit_bytes=40 * 1024 * 1024
        ),
    )(*(pltpu.with_memory_space_constraint(a, pltpu.HBM) for a in (by_piece, v_blocks, block_pos)), block_count)
    return out.reshape(half * 4 * rows, strip)


def solution(mesh):
    in_specs = (
        P("wide", "narrow"),
        P("narrow", "wide", None, None, None),
        P("narrow", "wide", None),
        P("narrow", "wide"),
    )
    out_specs = P("narrow", "wide")
    wide_size, narrow_size = mesh.shape["wide"], mesh.shape["narrow"]

    def program(t_amps, v_blocks, block_pos, block_count):
        width = t_amps.shape[1]
        if narrow_size == 2 and wide_size >= 16 and wide_size % 8 == 0:
            body = functools.partial(ring_shards, width, wide_size)
        else:
            body = functools.partial(dense_shards, width)
        run = jax.shard_map(body, mesh=mesh, in_specs=in_specs, out_specs=out_specs, check_vma=False)
        return run(t_amps, v_blocks, block_pos, block_count)

    return program
```

```python
import functools

import jax
import jax.numpy as jnp
from jax import lax
from jax.experimental import pallas as pl
from jax.experimental.pallas import tpu as pltpu
from jax.sharding import PartitionSpec as P

MESH = pl.DeviceIdType.MESH
PIECES = 4


def dense_shards(width, t_amps, v_blocks, block_pos, block_count):
    stored = v_blocks[0, 0]
    places = block_pos[0, 0]
    slot_count = block_count[0, 0]
    block_size = stored.shape[1]
    slot_total = stored.shape[0]
    row_blocks = t_amps.shape[1] // block_size
    col_blocks = width // (lax.axis_size("wide") * block_size)
    live_mask = (jnp.arange(slot_total, dtype=jnp.int32) < slot_count).astype(jnp.bfloat16)
    masked = stored * live_mask[:, None, None]
    dense_tile = jnp.zeros((row_blocks * col_blocks, block_size, block_size), jnp.bfloat16)
    dense_tile = dense_tile.at[places].add(masked)
    dense_tile = dense_tile.reshape(row_blocks, col_blocks, block_size, block_size)
    dense_tile = jnp.transpose(dense_tile, (0, 2, 1, 3)).reshape(row_blocks * block_size, col_blocks * block_size)
    gathered = lax.all_gather(t_amps, "wide", axis=0, tiled=True)
    partial_sum = jnp.dot(gathered, dense_tile, preferred_element_type=jnp.float32)
    return lax.psum_scatter(partial_sum, "narrow", scatter_dimension=0, tiled=True)


def ladder_kernel(depth, t, v_tile, pos, count, out, *scratch):
    total = (2 * depth - 1) * PIECES * 2
    bufs = [[scratch[2 * (b * PIECES + q):2 * (b * PIECES + q) + 2] for q in range(PIECES)] for b in range(2 * depth - 1)]
    (v_own, v_other, pos_own, count_own, pos_other, count_other, made, info_own, info_other, runs, part, core_in, y_out, far_in,
     lay_sem, local_sem, z_send, z_recv, x_send, x_recv, one_send, one_recv, core_send, core_recv, y_send, y_recv,
     far_send, far_recv) = scratch[total:]
    wide, core = lax.axis_index("wide"), lax.axis_index("narrow")
    z, y, x = wide // 4, (wide // 2) % 2, wide % 2
    up, down = (wide + 4, core), (wide - 4, core)
    across = (wide + 1 - 2 * x, core)
    beside = (wide + 2 - 4 * y, core)
    twin = (wide, 1 - core)
    facing = (wide + 2 - 4 * y, 1 - core)
    half = depth // 2
    pieces, row_blocks, chunk, unused = t.shape
    v = v_tile.at[0, 0]
    slots, size = v.shape[0], v.shape[1]
    col_blocks = out.shape[-1] // size
    has_up, has_down = z < depth - 1, z > 0
    at_end = jnp.logical_or(z == 0, z == depth - 1)
    first = row_blocks // 2
    second_cols = pl.ds(first, row_blocks - first)

    def copy(src, dst, send, recv, device):
        return pltpu.make_async_remote_copy(
            src_ref=src, dst_ref=dst, send_sem=send, recv_sem=recv, device_id=device, device_id_type=MESH
        )

    def guarded(cond, fn):
        if cond is None:
            fn()
        else:
            pl.when(cond)(fn)

    def both(a, b):
        return b if a is None else a if b is None else jnp.logical_and(a, b)

    def shards(k):
        if k == 0:
            return [(0, z, None, None)]
        return [(k, z - k, z >= k, 0), (depth - 1 + k, z + k, z + k < depth, 1)]

    def is_end(k, way):
        return at_end if k == 0 else (z == k) if way == 0 else (z + k == depth - 1)

    def onward(b, way):
        ups = [] if way == 1 or b == depth - 1 else [(0, up, has_up, b + 1)]
        downs = [] if way == 0 or b == 2 * depth - 2 else [(1, down, has_down, depth if b == 0 else b + 1)]
        return ups + downs

    def z_ref(b, kind, q):
        return bufs[b][q][0] if kind == 0 else bufs[b][q][1].at[second_cols]

    def z_copy(b, kind, q, move):
        direction, device, unused, landing = move
        src = t.at[q] if (b, kind) == (0, 0) else z_ref(b, kind, q)
        return copy(src, z_ref(landing, kind, q), z_send.at[direction, b, kind, q], z_recv.at[landing, kind, q], device)

    def x_copy(b, q, cols):
        mine_side, other_side = (ref.at[pl.ds(0, cols)] for ref in bufs[b][q])
        return copy(t.at[q] if b == 0 else mine_side, other_side, x_send.at[b, q], x_recv.at[b, q], across)

    def z_wait(b, kind, q):
        ref = z_ref(b, kind, q)
        copy(ref, ref, z_send.at[0, b, kind, q], z_recv.at[b, kind, q], up).wait_recv()

    def crossing(k, way, fn):
        if k == 0:
            fn(row_blocks)
        elif k == depth - 1:
            fn(first)
        else:
            pl.when(is_end(k, way))(lambda: fn(first))
            pl.when(jnp.logical_not(is_end(k, way)))(lambda: fn(row_blocks))

    def x_start(k, b, way, q):
        crossing(k, way, lambda cols: x_copy(b, q, cols).start())

    def x_wait(k, b, way, q):
        crossing(k, way, lambda cols: x_copy(b, q, cols).wait_recv())

    barrier = pltpu.get_barrier_semaphore()
    for device in (across, beside, twin, facing):
        pl.semaphore_signal(barrier, inc=1, device_id=device, device_id_type=MESH)
    pl.when(has_up)(lambda: pl.semaphore_signal(barrier, inc=1, device_id=up, device_id_type=MESH))
    pl.when(has_down)(lambda: pl.semaphore_signal(barrier, inc=1, device_id=down, device_id_type=MESH))
    lays = [pltpu.make_async_copy(t.at[q], bufs[0][q][0], lay_sem.at[q]) for q in range(pieces)]
    own_v = pltpu.make_async_copy(v, v_own, local_sem.at[0])
    own_p = pltpu.make_async_copy(pos, pos_own, local_sem.at[1])
    own_c = pltpu.make_async_copy(count, count_own, local_sem.at[2])
    for each in (*lays, own_v, own_p, own_c):
        each.start()
    pl.semaphore_wait(barrier, 4 + has_up.astype(jnp.int32) + has_down.astype(jnp.int32))

    vy = copy(v, v_other, one_send.at[0], one_recv.at[0], beside)
    py = copy(pos, pos_other, one_send.at[1], one_recv.at[1], beside)
    cy = copy(count, count_other, one_send.at[2], one_recv.at[2], beside)
    for q in range(pieces):
        for move in onward(0, None):
            guarded(move[2], lambda move=move: z_copy(0, 0, q, move).start())
        x_start(0, 0, None, q)
    py.start()
    cy.start()
    vy.start()

    def relay(k, kind, q):
        for b, zp, valid, way in shards(k):
            def run(b=b, way=way):
                z_wait(b, kind, q)
                for move in onward(b, way):
                    guarded(move[2], lambda move=move: z_copy(b, kind, q, move).start())
                if kind == 0:
                    x_start(k, b, way, q)

            guarded(valid if kind == 0 else both(valid, is_end(k, way)), run)

    def relay_own(q):
        x_wait(0, 0, None, q)

        def run():
            for move in onward(0, None):
                guarded(move[2], lambda move=move: z_copy(0, 1, q, move).start())

        pl.when(at_end)(run)

    def steps(k):
        if k == depth - 1:
            tail = [(1 - x, (1,), (0, 1))] + [(1 - x, (1,), (q,)) for q in range(2, pieces)]
            return [(x, (0,), tuple(range(pieces)))] + tail
        return [(pl.ds(0, 2), (0, 1), (q, q + 1)) for q in range(0, pieces, 2)]

    final = len(steps(depth - 1)) - 1

    def is_last(k, n):
        return (k, n) == (depth - 1, final)

    def span(k, n):
        sides, unused, qs = steps(k)[n]
        return sides, pl.ds(qs[0] * chunk, len(qs) * chunk)

    def core_copy(zp, strip, k, n):
        return copy(part.at[zp, strip, *span(k, n)], core_in.at[zp % half, strip, *span(k, n)],
                    core_send.at[zp, strip, n], core_recv.at[zp, strip, n], twin)

    def target(zp, k, n):
        return out.at[zp % half * 2 + y, *span(k, n)]

    def y_copy(zp, k, n):
        return copy(y_out.at[zp % half, *span(k, n)], target(zp, k, n), y_send.at[zp, n], y_recv.at[zp, n], beside)

    def far_copy(zp, slot, device):
        return copy(part.at[zp, 0, *span(depth - 1, final)], far_in.at[slot], far_send.at[slot], far_recv.at[slot], device)

    def mine(zp):
        return zp // half == core

    def chain(places, live, strip):
        place = places[0]
        shift = (col_blocks - 1).bit_length()
        row = place >> shift if col_blocks == 1 << shift else place // col_blocks
        along = jnp.broadcast_to(place - row * col_blocks, (slots, slots))
        down = along.T
        earlier = lax.broadcasted_iota(jnp.int32, (slots, slots), 0)
        at = lax.broadcasted_iota(jnp.int32, (slots, slots), 1)
        known = jnp.where(earlier < live[...], earlier + 1, 0)
        before = jnp.max(jnp.where(jnp.logical_and(down == along, earlier < at), known, 0), axis=0, keepdims=True)
        last = jnp.max(jnp.where(down == at, known, 0), axis=0, keepdims=True)
        for i, line in enumerate((row, before, last)):
            made[strip, i:i + 1, :slots] = line

    tables = ((v_other, info_other), (v_own, info_own))

    def products(b, zp, k, n, strips, unroll):
        unused, sides, qs = steps(k)[n]
        lines = len(sides) * len(qs) * chunk

        def slot(s, carry):
            for strip in strips:
                stored, info = tables[strip]
                at_row = info[0, s]
                left = jnp.concatenate([bufs[b][q][side][at_row] for side in sides for q in qs], axis=0)
                new = jnp.dot(left, stored[s], preferred_element_type=jnp.float32)
                runs[strip, s + 1, :lines] = new + runs[strip, info[1, s], :lines]
            return carry

        lax.fori_loop(0, slots, slot, 0, unroll=unroll)
        for strip in strips:
            info = tables[strip][1]
            for c in range(col_blocks):
                value = runs[strip, info[2, c], :lines]
                for i, side in enumerate(sides):
                    part[zp, strip, x if side == 0 else 1 - x, span(k, n)[1], c * size:(c + 1) * size] = (
                        value[i * len(qs) * chunk:(i + 1) * len(qs) * chunk])
            if is_last(k, n) and strip == 0:
                pl.when(mine(zp))(lambda: far_copy(zp, 0, beside).start())
                pl.when(jnp.logical_not(mine(zp)))(lambda: far_copy(zp, 1, facing).start())
            else:
                pl.when(jnp.logical_not(mine(zp)))(lambda: core_copy(zp, strip, k, n).start())

    def compute(k, n, ahead=None):
        for b, zp, valid, way in shards(k):
            def run(b=b, zp=zp, way=way):
                for q in steps(k)[n][2]:
                    if 0 < k < depth - 1 or n > 0 and k > 0:
                        x_wait(k, b, way, q)
                    if n > 0 and k == depth - 1:
                        z_wait(b, 1, q)
                if ahead is None:
                    products(b, zp, k, n, (0, 1), 16)
                else:
                    products(b, zp, k, n, (0,), 32)
                    finish(k, ahead, b)
                    products(b, zp, k, n, (1,), 32)

            guarded(valid, run)

    def finish(k, n, only=None):
        for b, zp, valid, way in shards(k):
            def run(zp=zp):
                if not is_last(k, n):
                    core_copy(zp, 0, k, n).wait_recv()
                    y_out[zp % half, *span(k, n)] = part[zp, 0, *span(k, n)] + core_in[zp % half, 0, *span(k, n)]
                    y_copy(zp, k, n).start()
                core_copy(zp, 1, k, n).wait_recv()
                out[zp % half * 2 + y, *span(k, n)] = part[zp, 1, *span(k, n)] + core_in[zp % half, 1, *span(k, n)]
                if is_last(k, n):
                    for slot in (0, 1):
                        far_copy(zp, slot, beside).wait_recv()
                    out[zp % half * 2 + 1 - y, *span(k, n)] = far_in[0] + far_in[1]

            if only is None:
                guarded(both(valid, mine(zp)), run)
            elif only == b:
                pl.when(mine(zp))(run)

    for strip in (0, 1):
        runs[strip, 0] = jnp.zeros(runs.shape[2:], jnp.float32)
    for q in range(pieces):
        relay(1, 0, q)
        relay_own(q)
    own_p.wait()
    own_c.wait()
    chain(pos_own, count_own, 1)
    py.wait_recv()
    cy.wait_recv()
    chain(pos_other, count_other, 0)
    for k in range(2, depth - 1):
        for q in range(pieces):
            relay(k - 1, 1, q)
            relay(k, 0, q)
    into = [pltpu.make_async_copy(made.at[strip], tables[strip][1], local_sem.at[3 + strip]) for strip in (0, 1)]
    for each in into:
        each.start()
    for each in into:
        each.wait()
    for each in (*lays, own_v):
        each.wait()
    vy.wait_recv()
    compute(0, 0)
    compute(0, 1)
    finish(0, 0)
    compute(1, 0)
    finish(0, 1)
    for q in range(pieces):
        relay(depth - 2, 1, q)
    compute(1, 1)
    finish(1, 0)
    finish(1, 1)
    for k in range(2, depth - 1):
        for n in range(len(steps(k))):
            if k == depth - 2:
                for q in range(2 * n, 2 * n + 2):
                    relay(depth - 1, 0, q)
            compute(k, n)
            if n == 0:
                finish(k, n)
    compute(depth - 1, 0)
    finish(depth - 2, 1)
    for n in range(1, final):
        compute(depth - 1, n)
        finish(depth - 1, n - 1)
    compute(depth - 1, final, final - 1)
    finish(depth - 1, final)

    vy.wait_send()
    py.wait_send()
    cy.wait_send()
    for k in range(depth):
        for b, zp, valid, way in shards(k):
            def run(b=b, zp=zp, way=way):
                for move in onward(b, way):
                    guarded(move[2], lambda move=move: [z_copy(b, 0, q, move).wait_send() for q in range(pieces)] and None)
                    guarded(both(is_end(k, way), move[2]), lambda move=move: [z_copy(b, 1, q, move).wait_send() for q in range(pieces)] and None)
                crossing(k, way, lambda cols: [x_copy(b, q, cols).wait_send() for q in range(pieces)] and None)
                other = jnp.logical_not(mine(zp))
                pl.when(other)(lambda: [core_copy(zp, j, k, n).wait_send() for j in (0, 1) for n in range(len(steps(k)))
                                        if j == 1 or not is_last(k, n)] and None)
                if k == depth - 1:
                    pl.when(other)(lambda: far_copy(zp, 1, facing).wait_send())
                    pl.when(mine(zp))(lambda: far_copy(zp, 0, beside).wait_send())
                pl.when(mine(zp))(lambda: [y_copy(zp, k, n).wait() for n in range(len(steps(k))) if not is_last(k, n)] and None)

            guarded(valid, run)


def ring_shards(width, wide_size, t_amps, v_blocks, block_pos, block_count):
    rows, columns = t_amps.shape
    slots, size = v_blocks.shape[2], v_blocks.shape[3]
    depth = wide_size // 4
    half, buffers = depth // 2, 2 * depth - 1
    strip = width // wide_size
    chunk = rows // PIECES
    lanes = -(-slots // 128) * 128
    by_piece = jnp.transpose(t_amps.reshape(PIECES, chunk, columns // size, size), (0, 2, 1, 3))
    bf16, f32, i32 = jnp.bfloat16, jnp.float32, jnp.int32
    dma = pltpu.SemaphoreType.DMA
    out = pl.pallas_call(
        functools.partial(ladder_kernel, depth),
        out_shape=jax.ShapeDtypeStruct((half * 2, 2, rows, strip), f32),
        in_specs=[
            pl.BlockSpec(memory_space=pltpu.HBM),
            pl.BlockSpec(memory_space=pltpu.HBM),
            pl.BlockSpec(memory_space=pltpu.HBM),
            pl.BlockSpec(memory_space=pltpu.HBM),
        ],
        out_specs=pl.BlockSpec(memory_space=pltpu.VMEM),
        scratch_shapes=[pltpu.VMEM((columns // size, chunk, size), bf16)] * (buffers * PIECES * 2) + [
            pltpu.VMEM((slots, size, size), bf16),
            pltpu.VMEM((slots, size, size), bf16),
            pltpu.VMEM(block_pos.shape, i32), pltpu.VMEM(block_count.shape, i32),
            pltpu.VMEM(block_pos.shape, i32), pltpu.VMEM(block_count.shape, i32),
            pltpu.VMEM((2, 8, lanes), i32),
            pltpu.SMEM((8, lanes), i32), pltpu.SMEM((8, lanes), i32),
            pltpu.VMEM((2, slots + 1, 4 * chunk, size), f32),
            pltpu.VMEM((depth, 2, 2, rows, strip), f32),
            pltpu.VMEM((half, 2, 2, rows, strip), f32),
            pltpu.VMEM((half, 2, rows, strip), f32),
            pltpu.VMEM((2, chunk, strip), f32),
            dma((PIECES,)),
            dma((5,)),
            dma((2, buffers, 2, PIECES)), dma((buffers, 2, PIECES)),
            dma((buffers, PIECES)), dma((buffers, PIECES)),
            dma((3,)), dma((3,)),
            dma((depth, 2, PIECES)), dma((depth, 2, PIECES)),
            dma((depth, PIECES)), dma((depth, PIECES)),
            dma((2,)), dma((2,)),
        ],
        compiler_params=pltpu.CompilerParams(
            collective_id=0, has_side_effects=True, vmem_limit_bytes=40 * 1024 * 1024
        ),
    )(*(pltpu.with_memory_space_constraint(a, pltpu.HBM) for a in (by_piece, v_blocks, block_pos)), block_count)
    return out.reshape(half * 4 * rows, strip)


def solution(mesh):
    in_specs = (
        P("wide", "narrow"),
        P("narrow", "wide", None, None, None),
        P("narrow", "wide", None),
        P("narrow", "wide"),
    )
    out_specs = P("narrow", "wide")
    wide_size, narrow_size = mesh.shape["wide"], mesh.shape["narrow"]

    def program(t_amps, v_blocks, block_pos, block_count):
        width = t_amps.shape[1]
        if narrow_size == 2 and wide_size >= 16 and wide_size % 8 == 0:
            body = functools.partial(ring_shards, width, wide_size)
        else:
            body = functools.partial(dense_shards, width)
        run = jax.shard_map(body, mesh=mesh, in_specs=in_specs, out_specs=out_specs, check_vma=False)
        return run(t_amps, v_blocks, block_pos, block_count)

    return program
```

```python
import functools

import jax
import jax.numpy as jnp
from jax import lax
from jax.experimental import pallas as pl
from jax.experimental.pallas import tpu as pltpu
from jax.sharding import PartitionSpec as P

MESH = pl.DeviceIdType.MESH
PIECES = 4


def dense_shards(width, t_amps, v_blocks, block_pos, block_count):
    stored = v_blocks[0, 0]
    places = block_pos[0, 0]
    slot_count = block_count[0, 0]
    block_size = stored.shape[1]
    slot_total = stored.shape[0]
    row_blocks = t_amps.shape[1] // block_size
    col_blocks = width // (lax.axis_size("wide") * block_size)
    live_mask = (jnp.arange(slot_total, dtype=jnp.int32) < slot_count).astype(jnp.bfloat16)
    masked = stored * live_mask[:, None, None]
    dense_tile = jnp.zeros((row_blocks * col_blocks, block_size, block_size), jnp.bfloat16)
    dense_tile = dense_tile.at[places].add(masked)
    dense_tile = dense_tile.reshape(row_blocks, col_blocks, block_size, block_size)
    dense_tile = jnp.transpose(dense_tile, (0, 2, 1, 3)).reshape(row_blocks * block_size, col_blocks * block_size)
    gathered = lax.all_gather(t_amps, "wide", axis=0, tiled=True)
    partial_sum = jnp.dot(gathered, dense_tile, preferred_element_type=jnp.float32)
    return lax.psum_scatter(partial_sum, "narrow", scatter_dimension=0, tiled=True)


def ladder_kernel(depth, t, v_tile, pos, count, out, *scratch):
    total = (2 * depth - 1) * PIECES * 2
    bufs = [[scratch[2 * (b * PIECES + q):2 * (b * PIECES + q) + 2] for q in range(PIECES)] for b in range(2 * depth - 1)]
    (v_own, v_other, pos_own, count_own, pos_other, count_other, made, info_own, info_other, runs, part, core_in, y_out, far_in,
     lay_sem, local_sem, z_send, z_recv, x_send, x_recv, one_send, one_recv, core_send, core_recv, y_send, y_recv,
     far_send, far_recv) = scratch[total:]
    wide, core = lax.axis_index("wide"), lax.axis_index("narrow")
    z, y, x = wide // 4, (wide // 2) % 2, wide % 2
    up, down = (wide + 4, core), (wide - 4, core)
    across = (wide + 1 - 2 * x, core)
    beside = (wide + 2 - 4 * y, core)
    twin = (wide, 1 - core)
    facing = (wide + 2 - 4 * y, 1 - core)
    half = depth // 2
    pieces, row_blocks, chunk, unused = t.shape
    v = v_tile.at[0, 0]
    slots, size = v.shape[0], v.shape[1]
    col_blocks = out.shape[-1] // size
    has_up, has_down = z < depth - 1, z > 0
    at_end = jnp.logical_or(z == 0, z == depth - 1)
    first = row_blocks // 2
    second_cols = pl.ds(first, row_blocks - first)

    def copy(src, dst, send, recv, device):
        return pltpu.make_async_remote_copy(
            src_ref=src, dst_ref=dst, send_sem=send, recv_sem=recv, device_id=device, device_id_type=MESH
        )

    def guarded(cond, fn):
        if cond is None:
            fn()
        else:
            pl.when(cond)(fn)

    def both(a, b):
        return b if a is None else a if b is None else jnp.logical_and(a, b)

    def shards(k):
        if k == 0:
            return [(0, z, None, None)]
        return [(k, z - k, z >= k, 0), (depth - 1 + k, z + k, z + k < depth, 1)]

    def is_end(k, way):
        return at_end if k == 0 else (z == k) if way == 0 else (z + k == depth - 1)

    def onward(b, way):
        ups = [] if way == 1 or b == depth - 1 else [(0, up, has_up, b + 1)]
        downs = [] if way == 0 or b == 2 * depth - 2 else [(1, down, has_down, depth if b == 0 else b + 1)]
        return ups + downs

    def z_ref(b, kind, q):
        return bufs[b][q][0] if kind == 0 else bufs[b][q][1].at[second_cols]

    def z_copy(b, kind, q, move):
        direction, device, unused, landing = move
        src = z_ref(b, kind, q)
        return copy(src, z_ref(landing, kind, q), z_send.at[direction, b, kind, q], z_recv.at[landing, kind, q], device)

    def x_copy(b, q, cols):
        mine_side, other_side = (ref.at[pl.ds(0, cols)] for ref in bufs[b][q])
        return copy(mine_side, other_side, x_send.at[b, q], x_recv.at[b, q], across)

    def z_wait(b, kind, q):
        ref = z_ref(b, kind, q)
        copy(ref, ref, z_send.at[0, b, kind, q], z_recv.at[b, kind, q], up).wait_recv()

    def crossing(k, way, fn):
        if k == 0:
            fn(row_blocks)
        elif k == depth - 1:
            fn(first)
        else:
            pl.when(is_end(k, way))(lambda: fn(first))
            pl.when(jnp.logical_not(is_end(k, way)))(lambda: fn(row_blocks))

    def x_start(k, b, way, q):
        crossing(k, way, lambda cols: x_copy(b, q, cols).start())

    def x_wait(k, b, way, q):
        crossing(k, way, lambda cols: x_copy(b, q, cols).wait_recv())

    barrier = pltpu.get_barrier_semaphore()
    for device in (across, beside, twin, facing):
        pl.semaphore_signal(barrier, inc=1, device_id=device, device_id_type=MESH)
    pl.when(has_up)(lambda: pl.semaphore_signal(barrier, inc=1, device_id=up, device_id_type=MESH))
    pl.when(has_down)(lambda: pl.semaphore_signal(barrier, inc=1, device_id=down, device_id_type=MESH))
    lays = [pltpu.make_async_copy(t.at[q], bufs[0][q][0], lay_sem.at[q]) for q in range(pieces)]
    own_v = pltpu.make_async_copy(v, v_own, local_sem.at[0])
    own_p = pltpu.make_async_copy(pos, pos_own, local_sem.at[1])
    own_c = pltpu.make_async_copy(count, count_own, local_sem.at[2])
    for each in (*lays, own_p, own_c):
        each.start()
    for lay in lays:
        lay.wait()
    pl.semaphore_wait(barrier, 4 + has_up.astype(jnp.int32) + has_down.astype(jnp.int32))

    vy = copy(v, v_other, one_send.at[0], one_recv.at[0], beside)
    py = copy(pos, pos_other, one_send.at[1], one_recv.at[1], beside)
    cy = copy(count, count_other, one_send.at[2], one_recv.at[2], beside)
    for q in range(pieces):
        for move in onward(0, None):
            guarded(move[2], lambda move=move: z_copy(0, 0, q, move).start())
        x_start(0, 0, None, q)
    py.start()
    cy.start()
    vy.start()
    own_v.start()

    def relay(k, kind, q):
        for b, zp, valid, way in shards(k):
            def run(b=b, way=way):
                z_wait(b, kind, q)
                for move in onward(b, way):
                    guarded(move[2], lambda move=move: z_copy(b, kind, q, move).start())
                if kind == 0:
                    x_start(k, b, way, q)

            guarded(valid if kind == 0 else both(valid, is_end(k, way)), run)

    def relay_own(q):
        x_wait(0, 0, None, q)

        def run():
            for move in onward(0, None):
                guarded(move[2], lambda move=move: z_copy(0, 1, q, move).start())

        pl.when(at_end)(run)

    def steps(k):
        if k == depth - 1:
            tail = [(1 - x, (1,), (0, 1))] + [(1 - x, (1,), (q,)) for q in range(2, pieces)]
            return [(x, (0,), tuple(range(pieces)))] + tail
        return [(pl.ds(0, 2), (0, 1), (q, q + 1)) for q in range(0, pieces, 2)]

    final = len(steps(depth - 1)) - 1

    def is_last(k, n):
        return (k, n) == (depth - 1, final)

    def span(k, n):
        sides, unused, qs = steps(k)[n]
        return sides, pl.ds(qs[0] * chunk, len(qs) * chunk)

    def core_copy(zp, strip, k, n):
        return copy(part.at[zp, strip, *span(k, n)], core_in.at[zp % half, strip, *span(k, n)],
                    core_send.at[zp, strip, n], core_recv.at[zp, strip, n], twin)

    def target(zp, k, n):
        return out.at[zp % half * 2 + y, *span(k, n)]

    def y_copy(zp, k, n):
        return copy(y_out.at[zp % half, *span(k, n)], target(zp, k, n), y_send.at[zp, n], y_recv.at[zp, n], beside)

    def far_copy(zp, slot, device):
        return copy(part.at[zp, 0, *span(depth - 1, final)], far_in.at[slot], far_send.at[slot], far_recv.at[slot], device)

    def mine(zp):
        return zp // half == core

    def chain(places, live, strip):
        place = places[0]
        shift = (col_blocks - 1).bit_length()
        row = place >> shift if col_blocks == 1 << shift else place // col_blocks
        along = jnp.broadcast_to(place - row * col_blocks, (slots, slots))
        down = along.T
        earlier = lax.broadcasted_iota(jnp.int32, (slots, slots), 0)
        at = lax.broadcasted_iota(jnp.int32, (slots, slots), 1)
        known = jnp.where(earlier < live[...], earlier + 1, 0)
        before = jnp.max(jnp.where(jnp.logical_and(down == along, earlier < at), known, 0), axis=0, keepdims=True)
        last = jnp.max(jnp.where(down == at, known, 0), axis=0, keepdims=True)
        for i, line in enumerate((row, before, last)):
            made[strip, i:i + 1, :slots] = line

    tables = ((v_other, info_other), (v_own, info_own))

    def products(b, zp, k, n, strips, unroll):
        unused, sides, qs = steps(k)[n]
        lines = len(sides) * len(qs) * chunk

        def slot(s, carry):
            for strip in strips:
                stored, info = tables[strip]
                at_row = info[0, s]
                left = jnp.concatenate([bufs[b][q][side][at_row] for side in sides for q in qs], axis=0)
                new = jnp.dot(left, stored[s], preferred_element_type=jnp.float32)
                runs[strip, s + 1, :lines] = new + runs[strip, info[1, s], :lines]
            return carry

        lax.fori_loop(0, slots, slot, 0, unroll=unroll)
        for strip in strips:
            info = tables[strip][1]
            for c in range(col_blocks):
                value = runs[strip, info[2, c], :lines]
                for i, side in enumerate(sides):
                    part[zp, strip, x if side == 0 else 1 - x, span(k, n)[1], c * size:(c + 1) * size] = (
                        value[i * len(qs) * chunk:(i + 1) * len(qs) * chunk])
            if is_last(k, n) and strip == 0:
                pl.when(mine(zp))(lambda: far_copy(zp, 0, beside).start())
                pl.when(jnp.logical_not(mine(zp)))(lambda: far_copy(zp, 1, facing).start())
            else:
                pl.when(jnp.logical_not(mine(zp)))(lambda: core_copy(zp, strip, k, n).start())

    def compute(k, n, ahead=None, strips=(0, 1), landed=False):
        for b, zp, valid, way in shards(k):
            def run(b=b, zp=zp, way=way):
                for q in steps(k)[n][2]:
                    if landed:
                        continue
                    if 0 < k < depth - 1 or n > 0 and k > 0:
                        x_wait(k, b, way, q)
                    if n > 0 and k == depth - 1:
                        z_wait(b, 1, q)
                if ahead is None:
                    products(b, zp, k, n, strips, 16)
                else:
                    products(b, zp, k, n, (0,), 32)
                    finish(k, ahead, b)
                    products(b, zp, k, n, (1,), 32)

            guarded(valid, run)

    def finish(k, n, only=None, strips=(0, 1)):
        for b, zp, valid, way in shards(k):
            def run(zp=zp):
                if 0 in strips and not is_last(k, n):
                    core_copy(zp, 0, k, n).wait_recv()
                    y_out[zp % half, *span(k, n)] = part[zp, 0, *span(k, n)] + core_in[zp % half, 0, *span(k, n)]
                    y_copy(zp, k, n).start()
                if 1 in strips:
                    core_copy(zp, 1, k, n).wait_recv()
                    out[zp % half * 2 + y, *span(k, n)] = part[zp, 1, *span(k, n)] + core_in[zp % half, 1, *span(k, n)]
                if is_last(k, n):
                    for slot in (0, 1):
                        far_copy(zp, slot, beside).wait_recv()
                    out[zp % half * 2 + 1 - y, *span(k, n)] = far_in[0] + far_in[1]

            if only is None:
                guarded(both(valid, mine(zp)), run)
            elif only == b:
                pl.when(mine(zp))(run)

    for strip in (0, 1):
        runs[strip, 0] = jnp.zeros(runs.shape[2:], jnp.float32)
    for q in range(pieces):
        relay(1, 0, q)
        relay_own(q)
    into = [pltpu.make_async_copy(made.at[strip], tables[strip][1], local_sem.at[3 + strip]) for strip in (0, 1)]
    own_p.wait()
    own_c.wait()
    chain(pos_own, count_own, 1)
    into[1].start()
    py.wait_recv()
    cy.wait_recv()
    chain(pos_other, count_other, 0)
    into[0].start()
    for each in (*into, own_v):
        each.wait()
    for n in range(len(steps(0))):
        compute(0, n, strips=(1,))
    for k in range(2, depth - 1):
        for q in range(pieces):
            relay(k - 1, 1, q)
            relay(k, 0, q)
    vy.wait_recv()
    compute(0, 0, strips=(0,), landed=True)
    compute(0, 1, strips=(0,), landed=True)
    finish(0, 0)
    compute(1, 0, strips=(0,))
    finish(0, 1)
    compute(1, 1, strips=(0,))
    finish(1, 0, strips=(0,))
    for q in range(pieces):
        relay(depth - 2, 1, q)
    finish(1, 1, strips=(0,))
    for n in range(len(steps(1))):
        compute(1, n, strips=(1,), landed=True)
    for n in range(len(steps(1))):
        finish(1, n, strips=(1,))
    for k in range(2, depth - 1):
        for n in range(len(steps(k))):
            if k == depth - 2:
                for q in range(2 * n, 2 * n + 2):
                    relay(depth - 1, 0, q)
            compute(k, n)
            if n == 0:
                finish(k, n)
    compute(depth - 1, 0)
    finish(depth - 2, 1)
    finish(depth - 1, 0)
    for n in range(1, final):
        compute(depth - 1, n)
        if n > 1:
            finish(depth - 1, n - 1)
    compute(depth - 1, final, final - 1)
    finish(depth - 1, final)

    vy.wait_send()
    py.wait_send()
    cy.wait_send()
    for k in range(depth):
        for b, zp, valid, way in shards(k):
            def run(b=b, zp=zp, way=way):
                for move in onward(b, way):
                    guarded(move[2], lambda move=move: [z_copy(b, 0, q, move).wait_send() for q in range(pieces)] and None)
                    guarded(both(is_end(k, way), move[2]), lambda move=move: [z_copy(b, 1, q, move).wait_send() for q in range(pieces)] and None)
                crossing(k, way, lambda cols: [x_copy(b, q, cols).wait_send() for q in range(pieces)] and None)
                other = jnp.logical_not(mine(zp))
                pl.when(other)(lambda: [core_copy(zp, j, k, n).wait_send() for j in (0, 1) for n in range(len(steps(k)))
                                        if j == 1 or not is_last(k, n)] and None)
                if k == depth - 1:
                    pl.when(other)(lambda: far_copy(zp, 1, facing).wait_send())
                    pl.when(mine(zp))(lambda: far_copy(zp, 0, beside).wait_send())
                pl.when(mine(zp))(lambda: [y_copy(zp, k, n).wait() for n in range(len(steps(k))) if not is_last(k, n)] and None)

            guarded(valid, run)


def ring_shards(width, wide_size, t_amps, v_blocks, block_pos, block_count):
    rows, columns = t_amps.shape
    slots, size = v_blocks.shape[2], v_blocks.shape[3]
    depth = wide_size // 4
    half, buffers = depth // 2, 2 * depth - 1
    strip = width // wide_size
    chunk = rows // PIECES
    lanes = -(-slots // 128) * 128
    by_piece = jnp.transpose(t_amps.reshape(PIECES, chunk, columns // size, size), (0, 2, 1, 3))
    bf16, f32, i32 = jnp.bfloat16, jnp.float32, jnp.int32
    dma = pltpu.SemaphoreType.DMA
    out = pl.pallas_call(
        functools.partial(ladder_kernel, depth),
        out_shape=jax.ShapeDtypeStruct((half * 2, 2, rows, strip), f32),
        in_specs=[
            pl.BlockSpec(memory_space=pltpu.HBM),
            pl.BlockSpec(memory_space=pltpu.HBM),
            pl.BlockSpec(memory_space=pltpu.HBM),
            pl.BlockSpec(memory_space=pltpu.HBM),
        ],
        out_specs=pl.BlockSpec(memory_space=pltpu.VMEM),
        scratch_shapes=[pltpu.VMEM((columns // size, chunk, size), bf16)] * (buffers * PIECES * 2) + [
            pltpu.VMEM((slots, size, size), bf16),
            pltpu.VMEM((slots, size, size), bf16),
            pltpu.VMEM(block_pos.shape, i32), pltpu.VMEM(block_count.shape, i32),
            pltpu.VMEM(block_pos.shape, i32), pltpu.VMEM(block_count.shape, i32),
            pltpu.VMEM((2, 8, lanes), i32),
            pltpu.SMEM((8, lanes), i32), pltpu.SMEM((8, lanes), i32),
            pltpu.VMEM((2, slots + 1, 4 * chunk, size), f32),
            pltpu.VMEM((depth, 2, 2, rows, strip), f32),
            pltpu.VMEM((half, 2, 2, rows, strip), f32),
            pltpu.VMEM((half, 2, rows, strip), f32),
            pltpu.VMEM((2, chunk, strip), f32),
            dma((PIECES,)),
            dma((5,)),
            dma((2, buffers, 2, PIECES)), dma((buffers, 2, PIECES)),
            dma((buffers, PIECES)), dma((buffers, PIECES)),
            dma((3,)), dma((3,)),
            dma((depth, 2, PIECES)), dma((depth, 2, PIECES)),
            dma((depth, PIECES)), dma((depth, PIECES)),
            dma((2,)), dma((2,)),
        ],
        compiler_params=pltpu.CompilerParams(
            collective_id=0, has_side_effects=True, vmem_limit_bytes=40 * 1024 * 1024
        ),
    )(*(pltpu.with_memory_space_constraint(a, pltpu.HBM) for a in (by_piece, v_blocks, block_pos)), block_count)
    return out.reshape(half * 4 * rows, strip)


def solution(mesh):
    in_specs = (
        P("wide", "narrow"),
        P("narrow", "wide", None, None, None),
        P("narrow", "wide", None),
        P("narrow", "wide"),
    )
    out_specs = P("narrow", "wide")
    wide_size, narrow_size = mesh.shape["wide"], mesh.shape["narrow"]

    def program(t_amps, v_blocks, block_pos, block_count):
        width = t_amps.shape[1]
        if narrow_size == 2 and wide_size >= 16 and wide_size % 8 == 0:
            body = functools.partial(ring_shards, width, wide_size)
        else:
            body = functools.partial(dense_shards, width)
        run = jax.shard_map(body, mesh=mesh, in_specs=in_specs, out_specs=out_specs, check_vma=False)
        return run(t_amps, v_blocks, block_pos, block_count)

    return program
```

```python
import functools

import jax
import jax.numpy as jnp
from jax import lax
from jax.experimental import pallas as pl
from jax.experimental.pallas import tpu as pltpu
from jax.sharding import PartitionSpec as P

MESH = pl.DeviceIdType.MESH
PIECES = 4


def dense_shards(width, t_amps, v_blocks, block_pos, block_count):
    stored = v_blocks[0, 0]
    places = block_pos[0, 0]
    slot_count = block_count[0, 0]
    block_size = stored.shape[1]
    slot_total = stored.shape[0]
    row_blocks = t_amps.shape[1] // block_size
    col_blocks = width // (lax.axis_size("wide") * block_size)
    live_mask = (jnp.arange(slot_total, dtype=jnp.int32) < slot_count).astype(jnp.bfloat16)
    masked = stored * live_mask[:, None, None]
    dense_tile = jnp.zeros((row_blocks * col_blocks, block_size, block_size), jnp.bfloat16)
    dense_tile = dense_tile.at[places].add(masked)
    dense_tile = dense_tile.reshape(row_blocks, col_blocks, block_size, block_size)
    dense_tile = jnp.transpose(dense_tile, (0, 2, 1, 3)).reshape(row_blocks * block_size, col_blocks * block_size)
    gathered = lax.all_gather(t_amps, "wide", axis=0, tiled=True)
    partial_sum = jnp.dot(gathered, dense_tile, preferred_element_type=jnp.float32)
    return lax.psum_scatter(partial_sum, "narrow", scatter_dimension=0, tiled=True)


def ladder_kernel(depth, t, v_tile, pos, count, out, *scratch):
    total = (2 * depth - 1) * PIECES * 2
    bufs = [[scratch[2 * (b * PIECES + q):2 * (b * PIECES + q) + 2] for q in range(PIECES)] for b in range(2 * depth - 1)]
    (v_own, v_other, pos_own, count_own, pos_other, count_other, made, info_own, info_other, runs, part, core_in, y_out, far_in,
     lay_sem, local_sem, z_send, z_recv, x_send, x_recv, one_send, one_recv, core_send, core_recv, y_send, y_recv,
     far_send, far_recv) = scratch[total:]
    wide, core = lax.axis_index("wide"), lax.axis_index("narrow")
    z, y, x = wide // 4, (wide // 2) % 2, wide % 2
    up, down = (wide + 4, core), (wide - 4, core)
    across = (wide + 1 - 2 * x, core)
    beside = (wide + 2 - 4 * y, core)
    twin = (wide, 1 - core)
    facing = (wide + 2 - 4 * y, 1 - core)
    half = depth // 2
    pieces, row_blocks, chunk, unused = t.shape
    v = v_tile.at[0, 0]
    slots, size = v.shape[0], v.shape[1]
    col_blocks = out.shape[-1] // size
    has_up, has_down = z < depth - 1, z > 0
    at_end = jnp.logical_or(z == 0, z == depth - 1)
    first = row_blocks // 2
    second_cols = pl.ds(first, row_blocks - first)

    def copy(src, dst, send, recv, device):
        return pltpu.make_async_remote_copy(
            src_ref=src, dst_ref=dst, send_sem=send, recv_sem=recv, device_id=device, device_id_type=MESH
        )

    def guarded(cond, fn):
        if cond is None:
            fn()
        else:
            pl.when(cond)(fn)

    def both(a, b):
        return b if a is None else a if b is None else jnp.logical_and(a, b)

    def shards(k):
        if k == 0:
            return [(0, z, None, None)]
        return [(k, z - k, z >= k, 0), (depth - 1 + k, z + k, z + k < depth, 1)]

    def is_end(k, way):
        return at_end if k == 0 else (z == k) if way == 0 else (z + k == depth - 1)

    def onward(b, way):
        ups = [] if way == 1 or b == depth - 1 else [(0, up, has_up, b + 1)]
        downs = [] if way == 0 or b == 2 * depth - 2 else [(1, down, has_down, depth if b == 0 else b + 1)]
        return ups + downs

    def z_ref(b, kind, q):
        return bufs[b][q][0] if kind == 0 else bufs[b][q][1].at[second_cols]

    def z_copy(b, kind, q, move):
        direction, device, unused, landing = move
        src = z_ref(b, kind, q)
        return copy(src, z_ref(landing, kind, q), z_send.at[direction, b, kind, q], z_recv.at[landing, kind, q], device)

    def x_copy(b, q, cols):
        mine_side, other_side = (ref.at[pl.ds(0, cols)] for ref in bufs[b][q])
        return copy(mine_side, other_side, x_send.at[b, q], x_recv.at[b, q], across)

    def z_wait(b, kind, q):
        ref = z_ref(b, kind, q)
        copy(ref, ref, z_send.at[0, b, kind, q], z_recv.at[b, kind, q], up).wait_recv()

    def crossing(k, way, fn):
        if k == 0:
            fn(row_blocks)
        elif k == depth - 1:
            fn(first)
        else:
            pl.when(is_end(k, way))(lambda: fn(first))
            pl.when(jnp.logical_not(is_end(k, way)))(lambda: fn(row_blocks))

    def x_start(k, b, way, q):
        crossing(k, way, lambda cols: x_copy(b, q, cols).start())

    def x_wait(k, b, way, q):
        crossing(k, way, lambda cols: x_copy(b, q, cols).wait_recv())

    barrier = pltpu.get_barrier_semaphore()
    for device in (across, beside, twin, facing):
        pl.semaphore_signal(barrier, inc=1, device_id=device, device_id_type=MESH)
    pl.when(has_up)(lambda: pl.semaphore_signal(barrier, inc=1, device_id=up, device_id_type=MESH))
    pl.when(has_down)(lambda: pl.semaphore_signal(barrier, inc=1, device_id=down, device_id_type=MESH))
    lays = [pltpu.make_async_copy(t.at[q], bufs[0][q][0], lay_sem.at[q]) for q in range(pieces)]
    own_v = pltpu.make_async_copy(v, v_own, local_sem.at[0])
    own_p = pltpu.make_async_copy(pos, pos_own, local_sem.at[1])
    own_c = pltpu.make_async_copy(count, count_own, local_sem.at[2])
    for each in (*lays, own_p, own_c):
        each.start()
    pl.semaphore_wait(barrier, 4 + has_up.astype(jnp.int32) + has_down.astype(jnp.int32))

    vy = copy(v, v_other, one_send.at[0], one_recv.at[0], beside)
    py = copy(pos, pos_other, one_send.at[1], one_recv.at[1], beside)
    cy = copy(count, count_other, one_send.at[2], one_recv.at[2], beside)
    for q in range(pieces):
        lays[q].wait()
        for move in onward(0, None):
            guarded(move[2], lambda move=move: z_copy(0, 0, q, move).start())
        x_start(0, 0, None, q)
    py.start()
    cy.start()
    vy.start()
    own_v.start()

    def relay(k, kind, q):
        for b, zp, valid, way in shards(k):
            def run(b=b, way=way):
                z_wait(b, kind, q)
                for move in onward(b, way):
                    guarded(move[2], lambda move=move: z_copy(b, kind, q, move).start())
                if kind == 0:
                    x_start(k, b, way, q)

            guarded(valid if kind == 0 else both(valid, is_end(k, way)), run)

    def relay_own(q):
        x_wait(0, 0, None, q)

        def run():
            for move in onward(0, None):
                guarded(move[2], lambda move=move: z_copy(0, 1, q, move).start())

        pl.when(at_end)(run)

    def steps(k):
        if k == depth - 1:
            tail = [(1 - x, (1,), (0, 1))] + [(1 - x, (1,), (q,)) for q in range(2, pieces)]
            return [(x, (0,), tuple(range(pieces)))] + tail
        return [(pl.ds(0, 2), (0, 1), (q, q + 1)) for q in range(0, pieces, 2)]

    final = len(steps(depth - 1)) - 1

    def is_last(k, n):
        return (k, n) == (depth - 1, final)

    def span(k, n):
        sides, unused, qs = steps(k)[n]
        return sides, pl.ds(qs[0] * chunk, len(qs) * chunk)

    def core_copy(zp, strip, k, n):
        return copy(part.at[zp, strip, *span(k, n)], core_in.at[zp % half, strip, *span(k, n)],
                    core_send.at[zp, strip, n], core_recv.at[zp, strip, n], twin)

    def target(zp, k, n):
        return out.at[zp % half * 2 + y, *span(k, n)]

    def y_copy(zp, k, n):
        return copy(y_out.at[zp % half, *span(k, n)], target(zp, k, n), y_send.at[zp, n], y_recv.at[zp, n], beside)

    def far_copy(zp, slot, device):
        return copy(part.at[zp, 0, *span(depth - 1, final)], far_in.at[slot], far_send.at[slot], far_recv.at[slot], device)

    def mine(zp):
        return zp // half == core

    def chain(places, live, strip):
        place = places[0]
        shift = (col_blocks - 1).bit_length()
        row = place >> shift if col_blocks == 1 << shift else place // col_blocks
        along = jnp.broadcast_to(place - row * col_blocks, (slots, slots))
        down = along.T
        earlier = lax.broadcasted_iota(jnp.int32, (slots, slots), 0)
        at = lax.broadcasted_iota(jnp.int32, (slots, slots), 1)
        known = jnp.where(earlier < live[...], earlier + 1, 0)
        before = jnp.max(jnp.where(jnp.logical_and(down == along, earlier < at), known, 0), axis=0, keepdims=True)
        last = jnp.max(jnp.where(down == at, known, 0), axis=0, keepdims=True)
        for i, line in enumerate((row, before, last)):
            made[strip, i:i + 1, :slots] = line

    tables = ((v_other, info_other), (v_own, info_own))

    def products(b, zp, k, n, strips, unroll):
        unused, sides, qs = steps(k)[n]
        lines = len(sides) * len(qs) * chunk

        def slot(s, carry):
            for strip in strips:
                stored, info = tables[strip]
                at_row = info[0, s]
                left = jnp.concatenate([bufs[b][q][side][at_row] for side in sides for q in qs], axis=0)
                new = jnp.dot(left, stored[s], preferred_element_type=jnp.float32)
                runs[strip, s + 1, :lines] = new + runs[strip, info[1, s], :lines]
            return carry

        lax.fori_loop(0, slots, slot, 0, unroll=unroll)
        for strip in strips:
            info = tables[strip][1]
            for c in range(col_blocks):
                value = runs[strip, info[2, c], :lines]
                for i, side in enumerate(sides):
                    part[zp, strip, x if side == 0 else 1 - x, span(k, n)[1], c * size:(c + 1) * size] = (
                        value[i * len(qs) * chunk:(i + 1) * len(qs) * chunk])
            if is_last(k, n) and strip == 0:
                pl.when(mine(zp))(lambda: far_copy(zp, 0, beside).start())
                pl.when(jnp.logical_not(mine(zp)))(lambda: far_copy(zp, 1, facing).start())
            else:
                pl.when(jnp.logical_not(mine(zp)))(lambda: core_copy(zp, strip, k, n).start())

    def compute(k, n, ahead=None, strips=(0, 1), landed=False):
        for b, zp, valid, way in shards(k):
            def run(b=b, zp=zp, way=way):
                for q in steps(k)[n][2]:
                    if landed:
                        continue
                    if 0 < k < depth - 1 or n > 0 and k > 0:
                        x_wait(k, b, way, q)
                    if n > 0 and k == depth - 1:
                        z_wait(b, 1, q)
                if ahead is None:
                    products(b, zp, k, n, strips, 16)
                else:
                    products(b, zp, k, n, (0,), 32)
                    finish(k, ahead, b)
                    products(b, zp, k, n, (1,), 32)

            guarded(valid, run)

    def finish(k, n, only=None, strips=(0, 1)):
        for b, zp, valid, way in shards(k):
            def run(zp=zp):
                if 0 in strips and not is_last(k, n):
                    core_copy(zp, 0, k, n).wait_recv()
                    y_out[zp % half, *span(k, n)] = part[zp, 0, *span(k, n)] + core_in[zp % half, 0, *span(k, n)]
                    y_copy(zp, k, n).start()
                if 1 in strips:
                    core_copy(zp, 1, k, n).wait_recv()
                    out[zp % half * 2 + y, *span(k, n)] = part[zp, 1, *span(k, n)] + core_in[zp % half, 1, *span(k, n)]
                if is_last(k, n):
                    for slot in (0, 1):
                        far_copy(zp, slot, beside).wait_recv()
                    out[zp % half * 2 + 1 - y, *span(k, n)] = far_in[0] + far_in[1]

            if only is None:
                guarded(both(valid, mine(zp)), run)
            elif only == b:
                pl.when(mine(zp))(run)

    for strip in (0, 1):
        runs[strip, 0] = jnp.zeros(runs.shape[2:], jnp.float32)
    for q in range(pieces):
        relay(1, 0, q)
        relay_own(q)
    into = [pltpu.make_async_copy(made.at[strip], tables[strip][1], local_sem.at[3 + strip]) for strip in (0, 1)]
    own_p.wait()
    own_c.wait()
    chain(pos_own, count_own, 1)
    into[1].start()
    py.wait_recv()
    cy.wait_recv()
    chain(pos_other, count_other, 0)
    into[0].start()
    for each in (*into, own_v):
        each.wait()
    for n in range(len(steps(0))):
        compute(0, n, strips=(1,))
    for k in range(2, depth - 1):
        for q in range(pieces):
            relay(k - 1, 1, q)
            relay(k, 0, q)
    vy.wait_recv()
    compute(0, 0, strips=(0,), landed=True)
    compute(0, 1, strips=(0,), landed=True)
    finish(0, 0)
    compute(1, 0, strips=(0,))
    finish(0, 1)
    compute(1, 1, strips=(0,))
    finish(1, 0, strips=(0,))
    for q in range(pieces):
        relay(depth - 2, 1, q)
    finish(1, 1, strips=(0,))
    for n in range(len(steps(1))):
        compute(1, n, strips=(1,), landed=True)
    for n in range(len(steps(1))):
        finish(1, n, strips=(1,))
    for k in range(2, depth - 1):
        for n in range(len(steps(k))):
            if k == depth - 2:
                for q in range(2 * n, 2 * n + 2):
                    relay(depth - 1, 0, q)
            compute(k, n)
            if n == 0:
                finish(k, n)
    compute(depth - 1, 0)
    finish(depth - 2, 1)
    finish(depth - 1, 0)
    for n in range(1, final):
        compute(depth - 1, n)
        if n > 1:
            finish(depth - 1, n - 1)
    compute(depth - 1, final, final - 1)
    finish(depth - 1, final)

    vy.wait_send()
    py.wait_send()
    cy.wait_send()
    for k in range(depth):
        for b, zp, valid, way in shards(k):
            def run(b=b, zp=zp, way=way):
                for move in onward(b, way):
                    guarded(move[2], lambda move=move: [z_copy(b, 0, q, move).wait_send() for q in range(pieces)] and None)
                    guarded(both(is_end(k, way), move[2]), lambda move=move: [z_copy(b, 1, q, move).wait_send() for q in range(pieces)] and None)
                crossing(k, way, lambda cols: [x_copy(b, q, cols).wait_send() for q in range(pieces)] and None)
                other = jnp.logical_not(mine(zp))
                pl.when(other)(lambda: [core_copy(zp, j, k, n).wait_send() for j in (0, 1) for n in range(len(steps(k)))
                                        if j == 1 or not is_last(k, n)] and None)
                if k == depth - 1:
                    pl.when(other)(lambda: far_copy(zp, 1, facing).wait_send())
                    pl.when(mine(zp))(lambda: far_copy(zp, 0, beside).wait_send())
                pl.when(mine(zp))(lambda: [y_copy(zp, k, n).wait() for n in range(len(steps(k))) if not is_last(k, n)] and None)

            guarded(valid, run)


def ring_shards(width, wide_size, t_amps, v_blocks, block_pos, block_count):
    rows, columns = t_amps.shape
    slots, size = v_blocks.shape[2], v_blocks.shape[3]
    depth = wide_size // 4
    half, buffers = depth // 2, 2 * depth - 1
    strip = width // wide_size
    chunk = rows // PIECES
    lanes = -(-slots // 128) * 128
    by_piece = jnp.transpose(t_amps.reshape(PIECES, chunk, columns // size, size), (0, 2, 1, 3))
    bf16, f32, i32 = jnp.bfloat16, jnp.float32, jnp.int32
    dma = pltpu.SemaphoreType.DMA
    out = pl.pallas_call(
        functools.partial(ladder_kernel, depth),
        out_shape=jax.ShapeDtypeStruct((half * 2, 2, rows, strip), f32),
        in_specs=[
            pl.BlockSpec(memory_space=pltpu.HBM),
            pl.BlockSpec(memory_space=pltpu.HBM),
            pl.BlockSpec(memory_space=pltpu.HBM),
            pl.BlockSpec(memory_space=pltpu.HBM),
        ],
        out_specs=pl.BlockSpec(memory_space=pltpu.VMEM),
        scratch_shapes=[pltpu.VMEM((columns // size, chunk, size), bf16)] * (buffers * PIECES * 2) + [
            pltpu.VMEM((slots, size, size), bf16),
            pltpu.VMEM((slots, size, size), bf16),
            pltpu.VMEM(block_pos.shape, i32), pltpu.VMEM(block_count.shape, i32),
            pltpu.VMEM(block_pos.shape, i32), pltpu.VMEM(block_count.shape, i32),
            pltpu.VMEM((2, 8, lanes), i32),
            pltpu.SMEM((8, lanes), i32), pltpu.SMEM((8, lanes), i32),
            pltpu.VMEM((2, slots + 1, 4 * chunk, size), f32),
            pltpu.VMEM((depth, 2, 2, rows, strip), f32),
            pltpu.VMEM((half, 2, 2, rows, strip), f32),
            pltpu.VMEM((half, 2, rows, strip), f32),
            pltpu.VMEM((2, chunk, strip), f32),
            dma((PIECES,)),
            dma((5,)),
            dma((2, buffers, 2, PIECES)), dma((buffers, 2, PIECES)),
            dma((buffers, PIECES)), dma((buffers, PIECES)),
            dma((3,)), dma((3,)),
            dma((depth, 2, PIECES)), dma((depth, 2, PIECES)),
            dma((depth, PIECES)), dma((depth, PIECES)),
            dma((2,)), dma((2,)),
        ],
        compiler_params=pltpu.CompilerParams(
            collective_id=0, has_side_effects=True, vmem_limit_bytes=40 * 1024 * 1024
        ),
    )(*(pltpu.with_memory_space_constraint(a, pltpu.HBM) for a in (by_piece, v_blocks, block_pos)), block_count)
    return out.reshape(half * 4 * rows, strip)


def solution(mesh):
    in_specs = (
        P("wide", "narrow"),
        P("narrow", "wide", None, None, None),
        P("narrow", "wide", None),
        P("narrow", "wide"),
    )
    out_specs = P("narrow", "wide")
    wide_size, narrow_size = mesh.shape["wide"], mesh.shape["narrow"]

    def program(t_amps, v_blocks, block_pos, block_count):
        width = t_amps.shape[1]
        if narrow_size == 2 and wide_size >= 16 and wide_size % 8 == 0:
            body = functools.partial(ring_shards, width, wide_size)
        else:
            body = functools.partial(dense_shards, width)
        run = jax.shard_map(body, mesh=mesh, in_specs=in_specs, out_specs=out_specs, check_vma=False)
        return run(t_amps, v_blocks, block_pos, block_count)

    return program
```

```python
import functools

import jax
import jax.numpy as jnp
from jax import lax
from jax.experimental import pallas as pl
from jax.experimental.pallas import tpu as pltpu
from jax.sharding import PartitionSpec as P

MESH = pl.DeviceIdType.MESH
PIECES = 4


def dense_shards(width, t_amps, v_blocks, block_pos, block_count):
    stored = v_blocks[0, 0]
    places = block_pos[0, 0]
    slot_count = block_count[0, 0]
    block_size = stored.shape[1]
    slot_total = stored.shape[0]
    row_blocks = t_amps.shape[1] // block_size
    col_blocks = width // (lax.axis_size("wide") * block_size)
    live_mask = (jnp.arange(slot_total, dtype=jnp.int32) < slot_count).astype(jnp.bfloat16)
    masked = stored * live_mask[:, None, None]
    dense_tile = jnp.zeros((row_blocks * col_blocks, block_size, block_size), jnp.bfloat16)
    dense_tile = dense_tile.at[places].add(masked)
    dense_tile = dense_tile.reshape(row_blocks, col_blocks, block_size, block_size)
    dense_tile = jnp.transpose(dense_tile, (0, 2, 1, 3)).reshape(row_blocks * block_size, col_blocks * block_size)
    gathered = lax.all_gather(t_amps, "wide", axis=0, tiled=True)
    partial_sum = jnp.dot(gathered, dense_tile, preferred_element_type=jnp.float32)
    return lax.psum_scatter(partial_sum, "narrow", scatter_dimension=0, tiled=True)


def ladder_kernel(depth, t, v_tile, pos, count, out, *scratch):
    total = (2 * depth - 1) * PIECES * 2
    bufs = [[scratch[2 * (b * PIECES + q):2 * (b * PIECES + q) + 2] for q in range(PIECES)] for b in range(2 * depth - 1)]
    (v_own, v_other, pos_own, count_own, pos_other, count_other, made, info_own, info_other, runs, part, core_in, y_out, far_in,
     lay_sem, local_sem, z_send, z_recv, x_send, x_recv, one_send, one_recv, core_send, core_recv, y_send, y_recv,
     far_send, far_recv) = scratch[total:]
    wide, core = lax.axis_index("wide"), lax.axis_index("narrow")
    z, y, x = wide // 4, (wide // 2) % 2, wide % 2
    up, down = (wide + 4, core), (wide - 4, core)
    across = (wide + 1 - 2 * x, core)
    beside = (wide + 2 - 4 * y, core)
    twin = (wide, 1 - core)
    facing = (wide + 2 - 4 * y, 1 - core)
    half = depth // 2
    pieces, row_blocks, chunk, unused = t.shape
    v = v_tile.at[0, 0]
    slots, size = v.shape[0], v.shape[1]
    col_blocks = out.shape[-1] // size
    has_up, has_down = z < depth - 1, z > 0
    at_end = jnp.logical_or(z == 0, z == depth - 1)
    first = row_blocks // 2
    second_cols = pl.ds(first, row_blocks - first)

    def copy(src, dst, send, recv, device):
        return pltpu.make_async_remote_copy(
            src_ref=src, dst_ref=dst, send_sem=send, recv_sem=recv, device_id=device, device_id_type=MESH
        )

    def guarded(cond, fn):
        if cond is None:
            fn()
        else:
            pl.when(cond)(fn)

    def both(a, b):
        return b if a is None else a if b is None else jnp.logical_and(a, b)

    def shards(k):
        if k == 0:
            return [(0, z, None, None)]
        return [(k, z - k, z >= k, 0), (depth - 1 + k, z + k, z + k < depth, 1)]

    def is_end(k, way):
        return at_end if k == 0 else (z == k) if way == 0 else (z + k == depth - 1)

    def onward(b, way):
        ups = [] if way == 1 or b == depth - 1 else [(0, up, has_up, b + 1)]
        downs = [] if way == 0 or b == 2 * depth - 2 else [(1, down, has_down, depth if b == 0 else b + 1)]
        return ups + downs

    def z_ref(b, kind, q):
        return bufs[b][q][0] if kind == 0 else bufs[b][q][1].at[second_cols]

    def z_copy(b, kind, q, move):
        direction, device, unused, landing = move
        src = z_ref(b, kind, q)
        return copy(src, z_ref(landing, kind, q), z_send.at[direction, b, kind, q], z_recv.at[landing, kind, q], device)

    def x_copy(b, q, cols):
        mine_side, other_side = (ref.at[pl.ds(0, cols)] for ref in bufs[b][q])
        return copy(mine_side, other_side, x_send.at[b, q], x_recv.at[b, q], across)

    def z_wait(b, kind, q):
        ref = z_ref(b, kind, q)
        copy(ref, ref, z_send.at[0, b, kind, q], z_recv.at[b, kind, q], up).wait_recv()

    def crossing(k, way, fn):
        if k == 0:
            fn(row_blocks)
        elif k == depth - 1:
            fn(first)
        else:
            pl.when(is_end(k, way))(lambda: fn(first))
            pl.when(jnp.logical_not(is_end(k, way)))(lambda: fn(row_blocks))

    def x_start(k, b, way, q):
        crossing(k, way, lambda cols: x_copy(b, q, cols).start())

    def x_wait(k, b, way, q):
        crossing(k, way, lambda cols: x_copy(b, q, cols).wait_recv())

    barrier = pltpu.get_barrier_semaphore()
    for device in (across, beside, twin, facing):
        pl.semaphore_signal(barrier, inc=1, device_id=device, device_id_type=MESH)
    pl.when(has_up)(lambda: pl.semaphore_signal(barrier, inc=1, device_id=up, device_id_type=MESH))
    pl.when(has_down)(lambda: pl.semaphore_signal(barrier, inc=1, device_id=down, device_id_type=MESH))
    lays = [pltpu.make_async_copy(t.at[q], bufs[0][q][0], lay_sem.at[q]) for q in range(pieces)]
    own_v = pltpu.make_async_copy(v, v_own, local_sem.at[0])
    own_p = pltpu.make_async_copy(pos, pos_own, local_sem.at[1])
    own_c = pltpu.make_async_copy(count, count_own, local_sem.at[2])
    for each in (*lays, own_p, own_c):
        each.start()
    pl.semaphore_wait(barrier, 4 + has_up.astype(jnp.int32) + has_down.astype(jnp.int32))

    vy = copy(v, v_other, one_send.at[0], one_recv.at[0], beside)
    py = copy(pos, pos_other, one_send.at[1], one_recv.at[1], beside)
    cy = copy(count, count_other, one_send.at[2], one_recv.at[2], beside)
    for q in range(pieces):
        lays[q].wait()
        for move in onward(0, None):
            guarded(move[2], lambda move=move: z_copy(0, 0, q, move).start())
        x_start(0, 0, None, q)
    py.start()
    cy.start()
    vy.start()
    own_v.start()

    def relay(k, kind, q):
        for b, zp, valid, way in shards(k):
            def run(b=b, way=way):
                z_wait(b, kind, q)
                for move in onward(b, way):
                    guarded(move[2], lambda move=move: z_copy(b, kind, q, move).start())
                if kind == 0:
                    x_start(k, b, way, q)

            guarded(valid if kind == 0 else both(valid, is_end(k, way)), run)

    def relay_own(q):
        x_wait(0, 0, None, q)

        def run():
            for move in onward(0, None):
                guarded(move[2], lambda move=move: z_copy(0, 1, q, move).start())

        pl.when(at_end)(run)

    def steps(k):
        if k == depth - 1:
            tail = [(1 - x, (1,), (0, 1))] + [(1 - x, (1,), (q,)) for q in range(2, pieces)]
            return [(x, (0,), tuple(range(pieces)))] + tail
        return [(pl.ds(0, 2), (0, 1), (q, q + 1)) for q in range(0, pieces, 2)]

    final = len(steps(depth - 1)) - 1

    def is_last(k, n):
        return (k, n) == (depth - 1, final)

    def span(k, n):
        sides, unused, qs = steps(k)[n]
        return sides, pl.ds(qs[0] * chunk, len(qs) * chunk)

    def core_copy(zp, strip, k, n):
        return copy(part.at[zp, strip, *span(k, n)], core_in.at[zp % half, strip, *span(k, n)],
                    core_send.at[zp, strip, n], core_recv.at[zp, strip, n], twin)

    def target(zp, k, n):
        return out.at[zp % half * 2 + y, *span(k, n)]

    def y_copy(zp, k, n):
        return copy(y_out.at[zp % half, *span(k, n)], target(zp, k, n), y_send.at[zp, n], y_recv.at[zp, n], beside)

    def far_copy(zp, slot, device):
        return copy(part.at[zp, 0, *span(depth - 1, final)], far_in.at[slot], far_send.at[slot], far_recv.at[slot], device)

    def mine(zp):
        return zp // half == core

    def chain(places, live, strip):
        place = places[0]
        shift = (col_blocks - 1).bit_length()
        row = place >> shift if col_blocks == 1 << shift else place // col_blocks
        along = jnp.broadcast_to(place - row * col_blocks, (slots, slots))
        down = along.T
        earlier = lax.broadcasted_iota(jnp.int32, (slots, slots), 0)
        at = lax.broadcasted_iota(jnp.int32, (slots, slots), 1)
        known = jnp.where(earlier < live[...], earlier + 1, 0)
        before = jnp.max(jnp.where(jnp.logical_and(down == along, earlier < at), known, 0), axis=0, keepdims=True)
        last = jnp.max(jnp.where(down == at, known, 0), axis=0, keepdims=True)
        for i, line in enumerate((row, before, last)):
            made[strip, i:i + 1, :slots] = line

    tables = ((v_other, info_other), (v_own, info_own))

    def products(b, zp, k, n, strips, unroll):
        unused, sides, qs = steps(k)[n]
        lines = len(sides) * len(qs) * chunk

        def slot(s, carry):
            for strip in strips:
                stored, info = tables[strip]
                at_row = info[0, s]
                left = jnp.concatenate([bufs[b][q][side][at_row] for side in sides for q in qs], axis=0)
                new = jnp.dot(left, stored[s], preferred_element_type=jnp.float32)
                runs[strip, s + 1, :lines] = new + runs[strip, info[1, s], :lines]
            return carry

        lax.fori_loop(0, slots, slot, 0, unroll=unroll)
        for strip in strips:
            info = tables[strip][1]
            for c in range(col_blocks):
                value = runs[strip, info[2, c], :lines]
                for i, side in enumerate(sides):
                    part[zp, strip, x if side == 0 else 1 - x, span(k, n)[1], c * size:(c + 1) * size] = (
                        value[i * len(qs) * chunk:(i + 1) * len(qs) * chunk])
            if is_last(k, n) and strip == 0:
                pl.when(mine(zp))(lambda: far_copy(zp, 0, beside).start())
                pl.when(jnp.logical_not(mine(zp)))(lambda: far_copy(zp, 1, facing).start())
            else:
                pl.when(jnp.logical_not(mine(zp)))(lambda: core_copy(zp, strip, k, n).start())

    def compute(k, n, ahead=None, strips=(0, 1), landed=False):
        for b, zp, valid, way in shards(k):
            def run(b=b, zp=zp, way=way):
                for q in steps(k)[n][2]:
                    if landed:
                        continue
                    if 0 < k < depth - 1 or n > 0 and k > 0:
                        x_wait(k, b, way, q)
                    if n > 0 and k == depth - 1:
                        z_wait(b, 1, q)
                if ahead is None:
                    products(b, zp, k, n, strips, 16)
                else:
                    products(b, zp, k, n, (0,), 32)
                    finish(k, ahead, b)
                    products(b, zp, k, n, (1,), 32)

            guarded(valid, run)

    def finish(k, n, only=None, strips=(0, 1)):
        for b, zp, valid, way in shards(k):
            def run(zp=zp):
                if 0 in strips and not is_last(k, n):
                    core_copy(zp, 0, k, n).wait_recv()
                    y_out[zp % half, *span(k, n)] = part[zp, 0, *span(k, n)] + core_in[zp % half, 0, *span(k, n)]
                    y_copy(zp, k, n).start()
                if 1 in strips:
                    core_copy(zp, 1, k, n).wait_recv()
                    out[zp % half * 2 + y, *span(k, n)] = part[zp, 1, *span(k, n)] + core_in[zp % half, 1, *span(k, n)]
                if is_last(k, n):
                    for slot in (0, 1):
                        far_copy(zp, slot, beside).wait_recv()
                    out[zp % half * 2 + 1 - y, *span(k, n)] = far_in[0] + far_in[1]

            if only is None:
                guarded(both(valid, mine(zp)), run)
            elif only == b:
                pl.when(mine(zp))(run)

    for strip in (0, 1):
        runs[strip, 0] = jnp.zeros(runs.shape[2:], jnp.float32)
    for q in range(pieces):
        relay(1, 0, q)
        relay_own(q)
    into = [pltpu.make_async_copy(made.at[strip], tables[strip][1], local_sem.at[3 + strip]) for strip in (0, 1)]
    own_p.wait()
    own_c.wait()
    chain(pos_own, count_own, 1)
    py.wait_recv()
    cy.wait_recv()
    chain(pos_other, count_other, 0)
    into[1].start()
    for each in (into[1], own_v):
        each.wait()
    for n in range(len(steps(0))):
        compute(0, n, strips=(1,))
    into[0].start()
    for k in range(2, depth - 1):
        for q in range(pieces):
            relay(k - 1, 1, q)
            relay(k, 0, q)
    into[0].wait()
    vy.wait_recv()
    compute(0, 0, strips=(0,), landed=True)
    compute(0, 1, strips=(0,), landed=True)
    finish(0, 0)
    compute(1, 0, strips=(0,))
    finish(0, 1)
    compute(1, 1, strips=(0,))
    finish(1, 0, strips=(0,))
    for q in range(pieces):
        relay(depth - 2, 1, q)
    finish(1, 1, strips=(0,))
    for n in range(len(steps(1))):
        compute(1, n, strips=(1,), landed=True)
    for n in range(len(steps(1))):
        finish(1, n, strips=(1,))
    for k in range(2, depth - 1):
        for n in range(len(steps(k))):
            if k == depth - 2:
                for q in range(2 * n, 2 * n + 2):
                    relay(depth - 1, 0, q)
            compute(k, n)
            if n == 0:
                finish(k, n)
    compute(depth - 1, 0)
    finish(depth - 2, 1)
    finish(depth - 1, 0)
    for n in range(1, final):
        compute(depth - 1, n)
        if n > 1:
            finish(depth - 1, n - 1)
    compute(depth - 1, final, final - 1)
    finish(depth - 1, final)

    vy.wait_send()
    py.wait_send()
    cy.wait_send()
    for k in range(depth):
        for b, zp, valid, way in shards(k):
            def run(b=b, zp=zp, way=way):
                for move in onward(b, way):
                    guarded(move[2], lambda move=move: [z_copy(b, 0, q, move).wait_send() for q in range(pieces)] and None)
                    guarded(both(is_end(k, way), move[2]), lambda move=move: [z_copy(b, 1, q, move).wait_send() for q in range(pieces)] and None)
                crossing(k, way, lambda cols: [x_copy(b, q, cols).wait_send() for q in range(pieces)] and None)
                other = jnp.logical_not(mine(zp))
                pl.when(other)(lambda: [core_copy(zp, j, k, n).wait_send() for j in (0, 1) for n in range(len(steps(k)))
                                        if j == 1 or not is_last(k, n)] and None)
                if k == depth - 1:
                    pl.when(other)(lambda: far_copy(zp, 1, facing).wait_send())
                    pl.when(mine(zp))(lambda: far_copy(zp, 0, beside).wait_send())
                pl.when(mine(zp))(lambda: [y_copy(zp, k, n).wait() for n in range(len(steps(k))) if not is_last(k, n)] and None)

            guarded(valid, run)


def ring_shards(width, wide_size, t_amps, v_blocks, block_pos, block_count):
    rows, columns = t_amps.shape
    slots, size = v_blocks.shape[2], v_blocks.shape[3]
    depth = wide_size // 4
    half, buffers = depth // 2, 2 * depth - 1
    strip = width // wide_size
    chunk = rows // PIECES
    lanes = -(-slots // 128) * 128
    by_piece = jnp.transpose(t_amps.reshape(PIECES, chunk, columns // size, size), (0, 2, 1, 3))
    bf16, f32, i32 = jnp.bfloat16, jnp.float32, jnp.int32
    dma = pltpu.SemaphoreType.DMA
    out = pl.pallas_call(
        functools.partial(ladder_kernel, depth),
        out_shape=jax.ShapeDtypeStruct((half * 2, 2, rows, strip), f32),
        in_specs=[
            pl.BlockSpec(memory_space=pltpu.HBM),
            pl.BlockSpec(memory_space=pltpu.HBM),
            pl.BlockSpec(memory_space=pltpu.HBM),
            pl.BlockSpec(memory_space=pltpu.HBM),
        ],
        out_specs=pl.BlockSpec(memory_space=pltpu.VMEM),
        scratch_shapes=[pltpu.VMEM((columns // size, chunk, size), bf16)] * (buffers * PIECES * 2) + [
            pltpu.VMEM((slots, size, size), bf16),
            pltpu.VMEM((slots, size, size), bf16),
            pltpu.VMEM(block_pos.shape, i32), pltpu.VMEM(block_count.shape, i32),
            pltpu.VMEM(block_pos.shape, i32), pltpu.VMEM(block_count.shape, i32),
            pltpu.VMEM((2, 8, lanes), i32),
            pltpu.SMEM((8, lanes), i32), pltpu.SMEM((8, lanes), i32),
            pltpu.VMEM((2, slots + 1, 4 * chunk, size), f32),
            pltpu.VMEM((depth, 2, 2, rows, strip), f32),
            pltpu.VMEM((half, 2, 2, rows, strip), f32),
            pltpu.VMEM((half, 2, rows, strip), f32),
            pltpu.VMEM((2, chunk, strip), f32),
            dma((PIECES,)),
            dma((5,)),
            dma((2, buffers, 2, PIECES)), dma((buffers, 2, PIECES)),
            dma((buffers, PIECES)), dma((buffers, PIECES)),
            dma((3,)), dma((3,)),
            dma((depth, 2, PIECES)), dma((depth, 2, PIECES)),
            dma((depth, PIECES)), dma((depth, PIECES)),
            dma((2,)), dma((2,)),
        ],
        compiler_params=pltpu.CompilerParams(
            collective_id=0, has_side_effects=True, vmem_limit_bytes=40 * 1024 * 1024
        ),
    )(*(pltpu.with_memory_space_constraint(a, pltpu.HBM) for a in (by_piece, v_blocks, block_pos)), block_count)
    return out.reshape(half * 4 * rows, strip)


def solution(mesh):
    in_specs = (
        P("wide", "narrow"),
        P("narrow", "wide", None, None, None),
        P("narrow", "wide", None),
        P("narrow", "wide"),
    )
    out_specs = P("narrow", "wide")
    wide_size, narrow_size = mesh.shape["wide"], mesh.shape["narrow"]

    def program(t_amps, v_blocks, block_pos, block_count):
        width = t_amps.shape[1]
        if narrow_size == 2 and wide_size >= 16 and wide_size % 8 == 0:
            body = functools.partial(ring_shards, width, wide_size)
        else:
            body = functools.partial(dense_shards, width)
        run = jax.shard_map(body, mesh=mesh, in_specs=in_specs, out_specs=out_specs, check_vma=False)
        return run(t_amps, v_blocks, block_pos, block_count)

    return program
```
